128 devices in a mesh: row: 8 (over x_hi, z), col: 16 (over x_lo, y, core).
Axes of the slice: x: 4 (x_hi: 2, x_lo: 2; x = x_hi * 2 + x_lo), y: 4, z: 4, core: 2. Of those that a mesh axis runs over, the one named last changes fastest.
Arguments:
- tokens: bfloat16 [4096, 2048], P(('row', 'col')), may hold values from -6 to 6
- routes: int32 [4096, 6], P(('row', 'col')), may hold values from 0 to 63, as said below
- router: bfloat16 [2048, 64], replicated, may hold values from -0.125 to 0.125
- w_in: bfloat16 [128, 2048, 1408], P(('row', 'col')), may hold values from -0.125 to 0.125
- w_out: bfloat16 [128, 704, 2048], P(('row', 'col')), may hold values from -0.15625 to 0.15625
- cache_prefill: bfloat16 [9216, 9216], P(('row', 'col')), may hold values from -6 to 6
- page_slot: int32 [9216], P(('row', 'col')), may hold values from 0 to 9215, as said below
Outputs:
- moe_out: bfloat16 [4096, 2048], P(('row', 'col'))
- cache_decode: bfloat16 [9216, 9216], P(('row', 'col'))
The draws below stay inside these ranges and needn't reach their ends.
Inputs may be any that keep to these rules, and one draw needn't show every extreme that they name: `routes`: each row names 6 different experts. In the rows of one device no expert is named more than 6 times, and one expert, the same for all devices, is named exactly 6 times in every device's rows. `page_slot`: A permutation of the page rows. Every device receives exactly 72 pages; at most 1 pages go from one device to one device, and some pair of devices reaches 1.
All inputs are finite; a program needn't handle non-finite values.
Results may differ from the reference program's by a relative error of at most 0.0065.
Values may be sent and summed in bfloat16 or wider, within the bound.
No kernel may reach another device: no remote copies, remote signals or barrier semaphores. Data moves between devices by JAX's collectives and lax.ppermute only.
A program may use at most 128 MiB of HBM per device.

```python
import jax
import jax.numpy as jnp
from jax import lax

D = 2048
FF = 1408
EXPERTS = 64
TOP = 6
TOK_DEV = 32
PAGE = 16
FFH = 704
KVW = 576
TOKENS = 4096
CAPE = 6
PAGES_DEV = 72
CPAGES = 9216
N_ROW = 8
N_COL = 16


def draw_routes(key, part):
    hot_expert = jax.random.randint(jax.random.fold_in(key, 11), (), 0, EXPERTS).astype(jnp.int32)
    block_count = TOKENS // TOK_DEV
    spare_count = TOP * TOK_DEV - CAPE

    def one_block(block_id):
        block_key = jax.random.fold_in(jax.random.fold_in(key, 12), block_id)
        first_key, second_key, third_key = jax.random.split(block_key, 3)
        others = (jnp.arange(EXPERTS - 1, dtype=jnp.int32) + hot_expert + 1) % EXPERTS
        candidates = jnp.repeat(others, CAPE, total_repeat_length=(EXPERTS - 1) * CAPE)
        chosen = jnp.sort(jax.random.permutation(first_key, (EXPERTS - 1) * CAPE)[:spare_count])
        sequence = jnp.concatenate([jnp.full((CAPE,), hot_expert, jnp.int32), candidates[chosen]])
        layout = sequence.reshape(TOP, TOK_DEV).T
        layout = layout[jax.random.permutation(second_key, TOK_DEV)]
        row_keys = jax.random.split(third_key, TOK_DEV)
        return jax.vmap(jax.random.permutation)(row_keys, layout)
    return jax.vmap(one_block)(jnp.arange(block_count)).reshape(TOKENS, TOP).astype(jnp.int32)


def draw_page_slot(key, part):
    device_count = CPAGES // PAGES_DEV
    base_share = PAGES_DEV // device_count
    extra_count = PAGES_DEV % device_count
    keys_four = jax.random.split(jax.random.fold_in(key, 21), 4)
    ranked = jax.random.permutation(keys_four[0], device_count)
    counts = base_share + (ranked < extra_count).astype(jnp.int32)
    run_ends = jnp.cumsum(counts)
    offsets = jnp.sum((run_ends[None, :] <= jnp.arange(PAGES_DEV)[:, None]).astype(jnp.int32), axis=1)
    base_shift = jax.random.permutation(keys_four[1], device_count)
    orders = jax.vmap(lambda number: jax.random.permutation(jax.random.fold_in(keys_four[2], number), PAGES_DEV))(jnp.arange(device_count))
    target = (base_shift[:, None] + offsets[orders]) % device_count
    within = jax.vmap(lambda number: jax.random.permutation(jax.random.fold_in(keys_four[3], number), PAGES_DEV))(jnp.arange(device_count))
    landing = within[target, orders]
    return (target * PAGES_DEV + landing).reshape(-1).astype(jnp.int32)


def levels(stream_key, extent, cuts, low, largest):
    factor_of = 1.0
    for position, blocks in cuts:
        draws = jax.random.uniform(jax.random.fold_in(jax.random.fold_in(stream_key, 6), position), (blocks,), jnp.float32, low / len(cuts), largest / len(cuts))
        factor_of = factor_of * jnp.repeat(jnp.exp(draws), extent[position] // blocks).reshape((-1,) + (1,) * (len(extent) - 1 - position))
    return factor_of


def scatter_about(own_key, dims, deviation, limit, pieces=(), kind=jnp.bfloat16):
    result = deviation * jax.random.normal(own_key, dims, jnp.float32)
    if pieces:
        result = result * levels(own_key, dims, pieces, -0.22, 0.18)
    return jnp.clip(result, -limit, limit).astype(kind)


def setup_inputs(seed: int = 0) -> dict:
    keys = jax.random.split(jax.random.key(seed), 8)
    tokens = scatter_about(keys[0], (TOKENS, D), 1.0, 6.0, ((0, 128),))
    routes = draw_routes(jax.random.fold_in(keys[7], 71), 0)
    router = scatter_about(keys[2], (D, EXPERTS), D ** -0.5, 0.125)
    w_in = scatter_about(keys[3], (2 * EXPERTS, D, 2 * FFH), D ** -0.5, 0.125, ((0, 128),))
    w_out = scatter_about(keys[4], (2 * EXPERTS, FFH, D), FF ** -0.5, 0.15625, ((0, 128),))
    cache_prefill = scatter_about(keys[5], (CPAGES, PAGE * KVW), 1.0, 6.0, ((0, 128),))
    page_slot = draw_page_slot(jax.random.fold_in(keys[7], 71), 0)
    return dict(tokens=tokens, routes=routes, router=router, w_in=w_in, w_out=w_out, cache_prefill=cache_prefill, page_slot=page_slot)


route_scale = 2.446


def gate_values_of(tokens, routes, router):
    logits = jnp.dot(tokens, router, preferred_element_type=jnp.float32)
    scores = jax.nn.sigmoid(logits)
    picked = jnp.take_along_axis(scores, routes, axis=1)
    return route_scale * picked / jnp.sum(picked, axis=1, keepdims=True)


def half_output(token_rows, w_first, w_second):
    gate_up = jnp.dot(token_rows, w_first, preferred_element_type=jnp.float32)
    hidden_width = w_second.shape[0]
    activated = (jax.nn.silu(gate_up[:, :hidden_width]) * gate_up[:, hidden_width:]).astype(jnp.bfloat16)
    return jnp.dot(activated, w_second, preferred_element_type=jnp.float32).astype(jnp.bfloat16)


def reference(tokens, routes, router, w_in, w_out, cache_prefill, page_slot):
    gate_values = gate_values_of(tokens, routes, router)
    flat_routes = routes.reshape(-1).astype(jnp.int32)
    ordering = jnp.argsort(flat_routes, stable=True).astype(jnp.int32)
    totals = jnp.zeros((EXPERTS,), jnp.int32).at[flat_routes].add(1)
    starts = (jnp.cumsum(totals) - totals).astype(jnp.int32)
    window_rows = CAPE * N_ROW * N_COL
    padded = jnp.concatenate([ordering, jnp.zeros((window_rows,), jnp.int32)])
    gate_flat = gate_values.reshape(-1)

    def one_expert(running, expert):
        offsets = jnp.arange(window_rows, dtype=jnp.int32)
        chosen = lax.dynamic_slice_in_dim(padded, starts[expert], window_rows)
        is_live = offsets < totals[expert]
        token_rows = tokens[chosen // TOP]
        part_low = half_output(token_rows, w_in[expert], w_out[expert])
        part_high = half_output(token_rows, w_in[EXPERTS + expert], w_out[EXPERTS + expert])
        merged = (part_low.astype(jnp.float32) + part_high.astype(jnp.float32)).astype(jnp.bfloat16)
        weight = jnp.where(is_live, gate_flat[chosen], jnp.zeros_like(gate_flat[chosen]))
        running = running.at[chosen // TOP].add(weight[:, None] * merged.astype(jnp.float32))
        return running, None

    summed, unused = lax.scan(one_expert, jnp.zeros((TOKENS, D), jnp.float32), jnp.arange(EXPERTS, dtype=jnp.int32))
    moe_out = summed.astype(jnp.bfloat16)
    cache_decode = jnp.zeros_like(cache_prefill).at[page_slot].set(cache_prefill)
    return (moe_out, cache_decode)
```

```python
import functools

import jax
import jax.numpy as jnp
from jax import lax
from jax.experimental import pallas as pl
from jax.experimental.pallas import tpu as pltpu
from jax.sharding import PartitionSpec as P

EXPERTS = 64
CAPE = 6
ROUTE_SCALE = 2.446
AXES = ("row", "col")
BF = jnp.bfloat16
F32 = jnp.float32
VM = pl.BlockSpec(memory_space=pltpu.VMEM)


UNITS = 3


def iota(shape, dim):
    return lax.broadcasted_iota(jnp.int32, shape, dim)


def onehot(cond):
    return jnp.where(cond, 1.0, 0.0).astype(BF)


def dispatch_kernel(routes_ref, tok_ref, out_ref):
    tok = tok_ref.shape[0]
    rows = out_ref.shape[0] // 2
    unit = out_ref.shape[1] // UNITS
    row = iota((rows, tok), 0)
    expert, sub = row >> 3, row & 7
    named = routes_ref[0:1, :] == expert
    for k in range(1, routes_ref.shape[0]):
        named = named | (routes_ref[k : k + 1, :] == expert)
    before = onehot(iota((tok, tok), 0) < iota((tok, tok), 1))
    rank = jnp.dot(onehot(named), before, preferred_element_type=F32).astype(jnp.int32)
    rank = jnp.where(named, rank, 99)
    main = onehot(rank == sub)
    last = tok_ref[:, UNITS * unit :]
    for u in range(UNITS):
        tail = onehot((sub >= CAPE) & (rank == sub + (2 * u - CAPE)))
        picked = jnp.dot(main, tok_ref[:, u * unit : (u + 1) * unit], preferred_element_type=F32)
        picked = picked + jnp.dot(tail, last, preferred_element_type=F32)
        picked = picked.astype(BF)
        out_ref[0:rows, u * unit : (u + 1) * unit] = picked
        out_ref[rows : 2 * rows, u * unit : (u + 1) * unit] = picked


def dispatch(routes_t, tokens):
    width = tokens.shape[1]
    return pl.pallas_call(
        dispatch_kernel,
        out_shape=jax.ShapeDtypeStruct((2 * EXPERTS * 8, width * CAPE // 8), BF),
        in_specs=[VM, VM],
        out_specs=VM,
        compiler_params=pltpu.CompilerParams(vmem_limit_bytes=24 << 20),
        cost_estimate=pl.CostEstimate(flops=10**8, bytes_accessed=4 * 10**6, transcendentals=0),
        name="dispatch",
    )(routes_t, tokens)


def gates_kernel(routes_ref, tok_ref, router_ref, out_ref):
    tok = tok_ref.shape[0]
    cols = out_ref.shape[1]
    logits = lax.dot_general(
        tok_ref[...], router_ref[...], (((1,), (1,)), ((), ())), preferred_element_type=F32
    )
    scores = jax.nn.sigmoid(logits)
    expert = iota((EXPERTS, tok), 0)
    named = routes_ref[0:1, :] == expert
    for k in range(1, routes_ref.shape[0]):
        named = named | (routes_ref[k : k + 1, :] == expert)
    unit = onehot(iota((tok, tok), 0) == iota((tok, tok), 1))
    mine = lax.dot_general(
        unit, onehot(named), (((1,), (1,)), ((), ())), preferred_element_type=F32
    )
    before = onehot(iota((tok, tok), 1) < iota((tok, tok), 0))
    rank = jnp.dot(before, mine.astype(BF), preferred_element_type=F32)
    rank = jnp.where(mine > 0.5, rank, 99.0)
    picked = jnp.where(mine > 0.5, scores, 0.0)
    gate = ROUTE_SCALE * picked / jnp.sum(picked, axis=1, keepdims=True)
    high = gate.astype(BF)
    low = (gate - high.astype(F32)).astype(BF)
    spread = onehot(((iota((EXPERTS, cols), 1) >> 3) & (EXPERTS - 1)) == iota((EXPERTS, cols), 0))
    rank = jnp.dot(rank.astype(BF), spread, preferred_element_type=F32).astype(jnp.int32)
    high = jnp.dot(high, spread, preferred_element_type=F32)
    low = jnp.dot(low, spread, preferred_element_type=F32)
    sub = iota((tok, cols), 1) & 7
    for u in range(UNITS + 1):
        if u == 0:
            keep = rank == sub
        else:
            keep = (sub >= CAPE) & (rank == sub + (2 * (u - 1) - CAPE))
        out_ref[2 * u * tok : (2 * u + 1) * tok, :] = jnp.where(keep, high, 0.0).astype(BF)
        out_ref[(2 * u + 1) * tok : (2 * u + 2) * tok, :] = jnp.where(keep, low, 0.0).astype(BF)


def gates(routes_t, tokens, router_t):
    tok = tokens.shape[0]
    return pl.pallas_call(
        gates_kernel,
        out_shape=jax.ShapeDtypeStruct((2 * (UNITS + 1) * tok, 2 * EXPERTS * 8), BF),
        in_specs=[VM, VM, VM],
        out_specs=VM,
        cost_estimate=pl.CostEstimate(flops=10**8, bytes_accessed=2 * 10**6, transcendentals=0),
        name="gates",
    )(routes_t, tokens, router_t)


def pages_out_kernel(slot_ref, cache_ref, out_ref, stack_ref):
    pages, width = cache_ref.shape
    rows, chunk = out_ref.shape
    for c in range(8):
        stack_ref[c * 128 : c * 128 + pages, :] = cache_ref[:, c * chunk : (c + 1) * chunk]
        stack_ref[c * 128 + pages : (c + 1) * 128, :] = jnp.zeros((128 - pages, chunk), BF)
    step = 256
    for b in range(rows // step):
        row = iota((step, 1024), 0) + b * step
        first = (row >> 3) * pages
        slot = slot_ref[...]
        hit = (slot >= first) & (slot < first + pages)
        hit = hit & ((iota((step, 1024), 1) >> 7) == (row & 7))
        got = jnp.dot(onehot(hit), stack_ref[...], preferred_element_type=F32)
        out_ref[b * step : (b + 1) * step, :] = got.astype(BF)


def pages_out(slot_row, cache, devices):
    width = cache.shape[1]
    return pl.pallas_call(
        pages_out_kernel,
        out_shape=jax.ShapeDtypeStruct((devices * 8, width // 8), BF),
        in_specs=[VM, VM],
        out_specs=VM,
        scratch_shapes=[pltpu.VMEM((1024, width // 8), BF)],
        compiler_params=pltpu.CompilerParams(vmem_limit_bytes=40 << 20),
        cost_estimate=pl.CostEstimate(flops=2 * 10**9, bytes_accessed=4 * 10**6, transcendentals=0),
        name="pages_out",
    )(slot_row, cache)


def pages_in_kernel(first_ref, slots_ref, got_ref, out_ref):
    pages, width = out_ref.shape
    rows, chunk = got_ref.shape
    devices = slots_ref.shape[0]
    local = slots_ref[...] - first_ref[0]
    hit = (local >= 0) & (local < pages)
    local = jnp.sum(jnp.where(hit, local + 1, 0), axis=1, keepdims=True).astype(F32)
    spread = (iota((devices, rows), 1) >> 3) == iota((devices, rows), 0)
    table = jnp.where(spread, local, 0.0).astype(BF)
    ones = jnp.ones((8, devices), BF)
    line = jnp.dot(ones, table, preferred_element_type=F32)[0:1, :].astype(jnp.int32)
    pad = -(-pages // 16) * 16
    sub = iota((pad, rows), 1) & 7
    same = line == iota((pad, rows), 0) + 1
    pick = jnp.concatenate([onehot(same & (sub == c)) for c in range(8)], axis=0)
    placed = jnp.dot(pick, got_ref[...], preferred_element_type=F32)
    for c in range(8):
        out_ref[:, c * chunk : (c + 1) * chunk] = placed[c * pad : c * pad + pages, :].astype(BF)


def pages_in(first, slots, got, pages):
    rows, chunk = got.shape
    return pl.pallas_call(
        pages_in_kernel,
        out_shape=jax.ShapeDtypeStruct((pages, chunk * 8), BF),
        in_specs=[pl.BlockSpec(memory_space=pltpu.SMEM), VM, VM],
        out_specs=VM,
        compiler_params=pltpu.CompilerParams(vmem_limit_bytes=40 << 20),
        cost_estimate=pl.CostEstimate(flops=2 * 10**9, bytes_accessed=4 * 10**6, transcendentals=0),
        name="pages_in",
    )(first, slots, got)


def experts_kernel(x_ref, w_in_ref, w_out_ref, out_ref):
    rows, packed = x_ref.shape
    unit = packed // UNITS
    hidden = w_out_ref.shape[0]
    block = 128
    row, col = iota((block, UNITS * block), 0), iota((block, UNITS * block), 1)
    sub = row & 7
    inner = col & (block - 1)
    gather = onehot(
        (sub < CAPE)
        & ((row >> 3) == (inner >> 3))
        & ((col >> 7) == (sub >> 1))
        & ((inner & 7) == CAPE + (sub & 1))
    )
    row, col = iota((UNITS * block, block), 0), iota((UNITS * block, block), 1)
    sub = row & 7
    scatter = onehot(
        (sub >= CAPE)
        & (((row & (block - 1)) >> 3) == (col >> 3))
        & ((col & 7) == 2 * (row >> 7) + sub - CAPE)
    )
    tails = []
    for b in range(rows // block):
        part = x_ref[b * block : (b + 1) * block, :]
        part = jnp.concatenate([part[:, u * unit : (u + 1) * unit] for u in range(UNITS)], axis=0)
        tails.append(jnp.dot(gather, part, preferred_element_type=F32).astype(BF))
    tail = jnp.concatenate(tails, axis=0)
    gate_up = jnp.dot(x_ref[...], w_in_ref[: UNITS * unit, :], preferred_element_type=F32)
    gate_up = gate_up + jnp.dot(tail, w_in_ref[UNITS * unit :, :], preferred_element_type=F32)
    act = (jax.nn.silu(gate_up[:, :hidden]) * gate_up[:, hidden:]).astype(BF)
    y = jnp.dot(act, w_out_ref[...], preferred_element_type=F32)
    for b in range(rows // block):
        part = y[b * block : (b + 1) * block, :]
        moved = jnp.dot(scatter, part[:, UNITS * unit :].astype(BF), preferred_element_type=F32)
        keep = (iota((block, unit), 0) & 7) < CAPE
        for u in range(UNITS):
            out_ref[b * block : (b + 1) * block, u * unit : (u + 1) * unit] = jnp.where(
                keep, part[:, u * unit : (u + 1) * unit], moved[u * block : (u + 1) * block, :]
            ).astype(BF)


def experts(x, w_in, w_out):
    rows, packed = x.shape
    step = 256
    once = pl.Buffered(1)
    return pl.pallas_call(
        experts_kernel,
        grid=(rows // step,),
        out_shape=jax.ShapeDtypeStruct(x.shape, BF),
        in_specs=[
            pl.BlockSpec((step, packed), lambda i: (i, 0)),
            pl.BlockSpec(w_in.shape, lambda i: (0, 0), pipeline_mode=once),
            pl.BlockSpec(w_out.shape, lambda i: (0, 0), pipeline_mode=once),
        ],
        out_specs=pl.BlockSpec((step, packed), lambda i: (i, 0)),
        compiler_params=pltpu.CompilerParams(vmem_limit_bytes=40 << 20),
        cost_estimate=pl.CostEstimate(
            flops=10**10, bytes_accessed=15 * 10**6, transcendentals=10**6
        ),
        name="experts",
    )(x, w_in, w_out)


def combine_kernel(gate_ref, got_ref, out_ref):
    tok = out_ref.shape[0]
    unit = got_ref.shape[1] // UNITS
    tail = jnp.zeros((2 * tok, unit), F32)
    for u in range(UNITS):
        part = got_ref[:, u * unit : (u + 1) * unit]
        main = jnp.dot(gate_ref[0 : 2 * tok, :], part, preferred_element_type=F32)
        out_ref[:, u * unit : (u + 1) * unit] = (main[:tok] + main[tok:]).astype(BF)
        tail = tail + jnp.dot(
            gate_ref[2 * tok * (u + 1) : 2 * tok * (u + 2), :], part, preferred_element_type=F32
        )
    out_ref[:, UNITS * unit :] = (tail[:tok] + tail[tok:]).astype(BF)


def combine(gate, got, tok, width):
    return pl.pallas_call(
        combine_kernel,
        out_shape=jax.ShapeDtypeStruct((tok, width), BF),
        in_specs=[VM, VM],
        out_specs=VM,
        cost_estimate=pl.CostEstimate(flops=10**9, bytes_accessed=4 * 10**6, transcendentals=0),
        name="combine",
    )(gate, got)


def swap(x):
    return lax.all_to_all(x, AXES, split_axis=0, concat_axis=0, tiled=True)


def per_device(tokens, routes, router, w_in, w_out, cache_prefill, page_slot):
    devices = lax.axis_size("row") * lax.axis_size("col")
    pages = page_slot.shape[0]
    slots = lax.all_gather(page_slot, AXES, axis=0, tiled=False)
    first = (lax.axis_index(AXES) * pages).astype(jnp.int32).reshape(1)
    routes_t = routes.T
    arrived = swap(dispatch(routes_t, tokens))
    gate = gates(routes_t, tokens, router.T)
    slot_row = jnp.pad(page_slot, (0, 128 - pages), constant_values=-1)
    slot_row = jnp.tile(slot_row, 8).reshape(1, 1024)
    moved = swap(pages_out(slot_row, cache_prefill, devices))
    returned = swap(experts(arrived, w_in[0], w_out[0]))
    cache_decode = pages_in(first, slots, moved, pages)
    moe_out = combine(gate, returned, tokens.shape[0], tokens.shape[1])
    return (moe_out, cache_decode)


def solution(mesh):
    in_specs = (
        P(AXES, None),
        P(AXES, None),
        P(),
        P(AXES, None, None),
        P(AXES, None, None),
        P(AXES, None),
        P(AXES),
    )
    out_specs = (P(AXES, None), P(AXES, None))
    return jax.shard_map(
        per_device, mesh=mesh, in_specs=in_specs, out_specs=out_specs, check_vma=False
    )
```

```python
import functools

import jax
import jax.numpy as jnp
from jax import lax
from jax.experimental import pallas as pl
from jax.experimental.pallas import tpu as pltpu
from jax.sharding import PartitionSpec as P

EXPERTS = 64
CAPE = 6
ROUTE_SCALE = 2.446
AXES = ("row", "col")
BF = jnp.bfloat16
F32 = jnp.float32
VM = pl.BlockSpec(memory_space=pltpu.VMEM)


UNITS = 3


def iota(shape, dim):
    return lax.broadcasted_iota(jnp.int32, shape, dim)


def onehot(cond):
    return jnp.where(cond, 1.0, 0.0).astype(BF)


def dispatch_kernel(routes_ref, tok_ref, out_ref):
    tok = tok_ref.shape[0]
    rows = out_ref.shape[0] // 2
    unit = out_ref.shape[1] // UNITS
    row = iota((rows, tok), 0)
    expert, sub = row >> 3, row & 7
    named = routes_ref[0:1, :] == expert
    for k in range(1, routes_ref.shape[0]):
        named = named | (routes_ref[k : k + 1, :] == expert)
    before = onehot(iota((tok, tok), 0) < iota((tok, tok), 1))
    rank = jnp.dot(onehot(named), before, preferred_element_type=F32).astype(jnp.int32)
    rank = jnp.where(named, rank, 99)
    main = onehot(rank == sub)
    last = tok_ref[:, UNITS * unit :]
    for u in range(UNITS):
        tail = onehot((sub >= CAPE) & (rank == sub + (2 * u - CAPE)))
        picked = jnp.dot(main, tok_ref[:, u * unit : (u + 1) * unit], preferred_element_type=F32)
        picked = picked + jnp.dot(tail, last, preferred_element_type=F32)
        picked = picked.astype(BF)
        out_ref[0:rows, u * unit : (u + 1) * unit] = picked
        out_ref[rows : 2 * rows, u * unit : (u + 1) * unit] = picked


def dispatch(routes_t, tokens):
    width = tokens.shape[1]
    return pl.pallas_call(
        dispatch_kernel,
        out_shape=jax.ShapeDtypeStruct((2 * EXPERTS * 8, width * CAPE // 8), BF),
        in_specs=[VM, VM],
        out_specs=VM,
        compiler_params=pltpu.CompilerParams(vmem_limit_bytes=24 << 20),
        cost_estimate=pl.CostEstimate(flops=10**8, bytes_accessed=4 * 10**6, transcendentals=0),
        name="dispatch",
    )(routes_t, tokens)


def gates_kernel(routes_ref, tok_ref, router_ref, out_ref):
    tok = tok_ref.shape[0]
    cols = out_ref.shape[1]
    logits = lax.dot_general(
        tok_ref[...], router_ref[...], (((1,), (1,)), ((), ())), preferred_element_type=F32
    )
    scores = jax.nn.sigmoid(logits)
    expert = iota((EXPERTS, tok), 0)
    named = routes_ref[0:1, :] == expert
    for k in range(1, routes_ref.shape[0]):
        named = named | (routes_ref[k : k + 1, :] == expert)
    unit = onehot(iota((tok, tok), 0) == iota((tok, tok), 1))
    mine = lax.dot_general(
        unit, onehot(named), (((1,), (1,)), ((), ())), preferred_element_type=F32
    )
    before = onehot(iota((tok, tok), 1) < iota((tok, tok), 0))
    rank = jnp.dot(before, mine.astype(BF), preferred_element_type=F32)
    rank = jnp.where(mine > 0.5, rank, 99.0)
    picked = jnp.where(mine > 0.5, scores, 0.0)
    gate = ROUTE_SCALE * picked / jnp.sum(picked, axis=1, keepdims=True)
    high = gate.astype(BF)
    low = (gate - high.astype(F32)).astype(BF)
    spread = onehot(((iota((EXPERTS, cols), 1) >> 3) & (EXPERTS - 1)) == iota((EXPERTS, cols), 0))
    rank = jnp.dot(rank.astype(BF), spread, preferred_element_type=F32).astype(jnp.int32)
    high = jnp.dot(high, spread, preferred_element_type=F32)
    low = jnp.dot(low, spread, preferred_element_type=F32)
    sub = iota((tok, cols), 1) & 7
    for u in range(UNITS + 1):
        if u == 0:
            keep = rank == sub
        else:
            keep = (sub >= CAPE) & (rank == sub + (2 * (u - 1) - CAPE))
        out_ref[2 * u * tok : (2 * u + 1) * tok, :] = jnp.where(keep, high, 0.0).astype(BF)
        out_ref[(2 * u + 1) * tok : (2 * u + 2) * tok, :] = jnp.where(keep, low, 0.0).astype(BF)


def gates(routes_t, tokens, router_t):
    tok = tokens.shape[0]
    return pl.pallas_call(
        gates_kernel,
        out_shape=jax.ShapeDtypeStruct((2 * (UNITS + 1) * tok, 2 * EXPERTS * 8), BF),
        in_specs=[VM, VM, VM],
        out_specs=VM,
        cost_estimate=pl.CostEstimate(flops=10**8, bytes_accessed=2 * 10**6, transcendentals=0),
        name="gates",
    )(routes_t, tokens, router_t)


def pages_out_kernel(slot_ref, cache_ref, out_ref, stack_ref):
    pages, width = cache_ref.shape
    rows = out_ref.shape[0]
    chunk = width // 8
    for c in range(8):
        stack_ref[c * 128 : c * 128 + pages, :] = cache_ref[:, c * chunk : (c + 1) * chunk]
        stack_ref[c * 128 + pages : (c + 1) * 128, :] = jnp.zeros((128 - pages, chunk), BF)
    step = 256
    for b in range(rows // step):
        row = iota((step, 1024), 0) + b * step
        first = (row >> 3) * pages
        slot = slot_ref[...]
        hit = (slot >= first) & (slot < first + pages)
        hit = hit & ((iota((step, 1024), 1) >> 7) == (row & 7))
        got = jnp.dot(onehot(hit), stack_ref[...], preferred_element_type=F32)
        out_ref[b * step : (b + 1) * step, :chunk] = got.astype(BF)
        landing = jnp.sum(jnp.where(hit, slot - first + 1, 0), axis=1, keepdims=True)
        landing = jnp.broadcast_to(landing.astype(F32), (step, 128))
        out_ref[b * step : (b + 1) * step, chunk:] = landing.astype(BF)


def pages_out(slot_row, cache, devices):
    width = cache.shape[1]
    return pl.pallas_call(
        pages_out_kernel,
        out_shape=jax.ShapeDtypeStruct((devices * 8, width // 8 + 128), BF),
        in_specs=[VM, VM],
        out_specs=VM,
        scratch_shapes=[pltpu.VMEM((1024, width // 8), BF)],
        compiler_params=pltpu.CompilerParams(vmem_limit_bytes=40 << 20),
        cost_estimate=pl.CostEstimate(flops=2 * 10**9, bytes_accessed=4 * 10**6, transcendentals=0),
        name="pages_out",
    )(slot_row, cache)


def pages_in_kernel(got_ref, out_ref):
    pages, width = out_ref.shape
    rows = got_ref.shape[0]
    chunk = width // 8
    landing = got_ref[:, chunk : chunk + 128].astype(F32)
    square = jnp.where(iota((128, 128), 0) == iota((128, 128), 1), 1.0, 0.0)
    line = [
        jnp.sum(landing[b * 128 : (b + 1) * 128, :] * square, axis=0, keepdims=True)
        for b in range(rows // 128)
    ]
    line = jnp.concatenate(line, axis=1).astype(jnp.int32)
    pad = -(-pages // 16) * 16
    sub = iota((pad, rows), 1) & 7
    same = line == iota((pad, rows), 0) + 1
    pick = jnp.concatenate([onehot(same & (sub == c)) for c in range(8)], axis=0)
    placed = jnp.dot(pick, got_ref[:, :chunk], preferred_element_type=F32)
    for c in range(8):
        out_ref[:, c * chunk : (c + 1) * chunk] = placed[c * pad : c * pad + pages, :].astype(BF)


def pages_in(got, pages, width):
    return pl.pallas_call(
        pages_in_kernel,
        out_shape=jax.ShapeDtypeStruct((pages, width), BF),
        in_specs=[VM],
        out_specs=VM,
        compiler_params=pltpu.CompilerParams(vmem_limit_bytes=40 << 20),
        cost_estimate=pl.CostEstimate(flops=2 * 10**9, bytes_accessed=4 * 10**6, transcendentals=0),
        name="pages_in",
    )(got)


def experts_kernel(x_ref, w_in_ref, w_out_ref, out_ref):
    rows, packed = x_ref.shape
    unit = packed // UNITS
    hidden = w_out_ref.shape[0]
    block = 128
    row, col = iota((block, UNITS * block), 0), iota((block, UNITS * block), 1)
    sub = row & 7
    inner = col & (block - 1)
    gather = onehot(
        (sub < CAPE)
        & ((row >> 3) == (inner >> 3))
        & ((col >> 7) == (sub >> 1))
        & ((inner & 7) == CAPE + (sub & 1))
    )
    row, col = iota((UNITS * block, block), 0), iota((UNITS * block, block), 1)
    sub = row & 7
    scatter = onehot(
        (sub >= CAPE)
        & (((row & (block - 1)) >> 3) == (col >> 3))
        & ((col & 7) == 2 * (row >> 7) + sub - CAPE)
    )
    tails = []
    for b in range(rows // block):
        part = x_ref[b * block : (b + 1) * block, :]
        part = jnp.concatenate([part[:, u * unit : (u + 1) * unit] for u in range(UNITS)], axis=0)
        tails.append(jnp.dot(gather, part, preferred_element_type=F32).astype(BF))
    tail = jnp.concatenate(tails, axis=0)
    gate_up = jnp.dot(x_ref[...], w_in_ref[: UNITS * unit, :], preferred_element_type=F32)
    gate_up = gate_up + jnp.dot(tail, w_in_ref[UNITS * unit :, :], preferred_element_type=F32)
    act = (jax.nn.silu(gate_up[:, :hidden]) * gate_up[:, hidden:]).astype(BF)
    y = jnp.dot(act, w_out_ref[...], preferred_element_type=F32)
    for b in range(rows // block):
        part = y[b * block : (b + 1) * block, :]
        moved = jnp.dot(scatter, part[:, UNITS * unit :].astype(BF), preferred_element_type=F32)
        keep = (iota((block, unit), 0) & 7) < CAPE
        for u in range(UNITS):
            out_ref[b * block : (b + 1) * block, u * unit : (u + 1) * unit] = jnp.where(
                keep, part[:, u * unit : (u + 1) * unit], moved[u * block : (u + 1) * block, :]
            ).astype(BF)


def experts(x, w_in, w_out):
    rows, packed = x.shape
    step = 256
    once = pl.Buffered(1)
    return pl.pallas_call(
        experts_kernel,
        grid=(rows // step,),
        out_shape=jax.ShapeDtypeStruct(x.shape, BF),
        in_specs=[
            pl.BlockSpec((step, packed), lambda i: (i, 0)),
            pl.BlockSpec(w_in.shape, lambda i: (0, 0), pipeline_mode=once),
            pl.BlockSpec(w_out.shape, lambda i: (0, 0), pipeline_mode=once),
        ],
        out_specs=pl.BlockSpec((step, packed), lambda i: (i, 0)),
        compiler_params=pltpu.CompilerParams(vmem_limit_bytes=40 << 20),
        cost_estimate=pl.CostEstimate(
            flops=10**10, bytes_accessed=15 * 10**6, transcendentals=10**6
        ),
        name="experts",
    )(x, w_in, w_out)


def combine_kernel(gate_ref, got_ref, out_ref):
    tok = out_ref.shape[0]
    unit = got_ref.shape[1] // UNITS
    tail = jnp.zeros((2 * tok, unit), F32)
    for u in range(UNITS):
        part = got_ref[:, u * unit : (u + 1) * unit]
        main = jnp.dot(gate_ref[0 : 2 * tok, :], part, preferred_element_type=F32)
        out_ref[:, u * unit : (u + 1) * unit] = (main[:tok] + main[tok:]).astype(BF)
        tail = tail + jnp.dot(
            gate_ref[2 * tok * (u + 1) : 2 * tok * (u + 2), :], part, preferred_element_type=F32
        )
    out_ref[:, UNITS * unit :] = (tail[:tok] + tail[tok:]).astype(BF)


def combine(gate, got, tok, width):
    return pl.pallas_call(
        combine_kernel,
        out_shape=jax.ShapeDtypeStruct((tok, width), BF),
        in_specs=[VM, VM],
        out_specs=VM,
        cost_estimate=pl.CostEstimate(flops=10**9, bytes_accessed=4 * 10**6, transcendentals=0),
        name="combine",
    )(gate, got)


def swap(x):
    return lax.all_to_all(x, AXES, split_axis=0, concat_axis=0, tiled=True)


def per_device(tokens, routes, router, w_in, w_out, cache_prefill, page_slot):
    devices = lax.axis_size("row") * lax.axis_size("col")
    pages = page_slot.shape[0]
    routes_t = routes.T
    arrived = swap(dispatch(routes_t, tokens))
    gate = gates(routes_t, tokens, router.T)
    slot_row = jnp.pad(page_slot, (0, 128 - pages), constant_values=-1)
    slot_row = jnp.tile(slot_row, 8).reshape(1, 1024)
    moved = swap(pages_out(slot_row, cache_prefill, devices))
    returned = swap(experts(arrived, w_in[0], w_out[0]))
    cache_decode = pages_in(moved, pages, cache_prefill.shape[1])
    moe_out = combine(gate, returned, tokens.shape[0], tokens.shape[1])
    return (moe_out, cache_decode)


def solution(mesh):
    in_specs = (
        P(AXES, None),
        P(AXES, None),
        P(),
        P(AXES, None, None),
        P(AXES, None, None),
        P(AXES, None),
        P(AXES),
    )
    out_specs = (P(AXES, None), P(AXES, None))
    return jax.shard_map(
        per_device, mesh=mesh, in_specs=in_specs, out_specs=out_specs, check_vma=False
    )
```

```python
import functools

import jax
import jax.numpy as jnp
from jax import lax
from jax.experimental import pallas as pl
from jax.experimental.pallas import tpu as pltpu
from jax.sharding import PartitionSpec as P

EXPERTS = 64
CAPE = 6
CHUNKS = 2
ROUTE_SCALE = 2.446
AXES = ("row", "col")
SWAP = ("col", "row")
BF = jnp.bfloat16
F32 = jnp.float32
VM = pl.BlockSpec(memory_space=pltpu.VMEM)


UNITS = 3


def iota(shape, dim):
    return lax.broadcasted_iota(jnp.int32, shape, dim)


def onehot(cond):
    return jnp.where(cond, 1.0, 0.0).astype(BF)


def expert_of(message):
    return ((message & 3) << 4) + (message >> 3)


def dispatch_kernel(routes_hbm, tok_hbm, out_hbm, routes_ref, tok_ref, buf_ref, in_sem, out_sem):
    tok = tok_ref.shape[0]
    rows = EXPERTS * 8
    unit = buf_ref.shape[3]
    load_routes = pltpu.make_async_copy(routes_hbm, routes_ref, in_sem.at[0])
    load_tok = pltpu.make_async_copy(tok_hbm, tok_ref, in_sem.at[1])
    load_routes.start()
    load_tok.start()
    load_routes.wait()
    row = iota((rows, tok), 0)
    expert, sub = expert_of(((row >> 5) << 3) + ((row >> 3) & 3)), row & 7
    named = routes_ref[0:1, :] == expert
    for k in range(1, routes_ref.shape[0]):
        named = named | (routes_ref[k : k + 1, :] == expert)
    before = onehot(iota((tok, tok), 0) < iota((tok, tok), 1))
    rank = jnp.dot(onehot(named), before, preferred_element_type=F32).astype(jnp.int32)
    rank = jnp.where(named, rank, 99)
    main = onehot(rank == sub)
    load_tok.wait()
    last = tok_ref[:, UNITS * unit :]
    stores = []
    for u in range(UNITS):
        tail = onehot((sub >= CAPE) & (rank == sub + (2 * u - CAPE)))
        picked = jnp.dot(main, tok_ref[:, u * unit : (u + 1) * unit], preferred_element_type=F32)
        picked = picked + jnp.dot(tail, last, preferred_element_type=F32)
        buf_ref[u] = picked.astype(BF).reshape(buf_ref.shape[1:])
        for half in range(2):
            store = pltpu.make_async_copy(
                buf_ref.at[u],
                out_hbm.at[:, half, :, u * unit : (u + 1) * unit],
                out_sem.at[2 * u + half],
            )
            store.start()
            stores.append(store)
    for store in stores:
        store.wait()


def dispatch(routes_t, tokens):
    width = tokens.shape[1]
    unit = width * CAPE // 8 // UNITS
    hbm = pl.BlockSpec(memory_space=pltpu.HBM)
    out = pl.pallas_call(
        dispatch_kernel,
        out_shape=jax.ShapeDtypeStruct((16, 2, 32, UNITS * unit), BF),
        in_specs=[hbm, hbm],
        out_specs=hbm,
        scratch_shapes=[
            pltpu.VMEM(routes_t.shape, jnp.int32),
            pltpu.VMEM(tokens.shape, BF),
            pltpu.VMEM((UNITS, 16, 32, unit), BF),
            pltpu.SemaphoreType.DMA((2,)),
            pltpu.SemaphoreType.DMA((2 * UNITS,)),
        ],
        cost_estimate=pl.CostEstimate(flops=10**8, bytes_accessed=4 * 10**6, transcendentals=0),
        name="dispatch",
    )(routes_t, tokens)
    return out.reshape(2 * EXPERTS * 8, UNITS * unit)


def gates_kernel(routes_ref, tok_ref, router_ref, out_ref):
    tok = tok_ref.shape[0]
    cols = out_ref.shape[1]
    logits = lax.dot_general(
        tok_ref[...], router_ref[...], (((1,), (1,)), ((), ())), preferred_element_type=F32
    )
    scores = jax.nn.sigmoid(logits)
    expert = iota((EXPERTS, tok), 0)
    named = routes_ref[0:1, :] == expert
    for k in range(1, routes_ref.shape[0]):
        named = named | (routes_ref[k : k + 1, :] == expert)
    unit = onehot(iota((tok, tok), 0) == iota((tok, tok), 1))
    mine = lax.dot_general(
        unit, onehot(named), (((1,), (1,)), ((), ())), preferred_element_type=F32
    )
    before = onehot(iota((tok, tok), 1) < iota((tok, tok), 0))
    rank = jnp.dot(before, mine.astype(BF), preferred_element_type=F32)
    rank = jnp.where(mine > 0.5, rank, 99.0)
    picked = jnp.where(mine > 0.5, scores, 0.0)
    gate = ROUTE_SCALE * picked / jnp.sum(picked, axis=1, keepdims=True)
    high = gate.astype(BF)
    low = (gate - high.astype(F32)).astype(BF)
    spread = onehot(expert_of(iota((EXPERTS, cols), 1) >> 3) == iota((EXPERTS, cols), 0))
    rank = jnp.dot(rank.astype(BF), spread, preferred_element_type=F32).astype(jnp.int32)
    high = jnp.dot(high, spread, preferred_element_type=F32)
    low = jnp.dot(low, spread, preferred_element_type=F32)
    sub = iota((tok, cols), 1) & 7
    for u in range(UNITS + 1):
        if u == 0:
            keep = rank == sub
        else:
            keep = (sub >= CAPE) & (rank == sub + (2 * (u - 1) - CAPE))
        out_ref[2 * u * tok : (2 * u + 1) * tok, :] = jnp.where(keep, high, 0.0).astype(BF)
        out_ref[(2 * u + 1) * tok : (2 * u + 2) * tok, :] = jnp.where(keep, low, 0.0).astype(BF)


def gates(routes_t, tokens, router_t):
    tok = tokens.shape[0]
    return pl.pallas_call(
        gates_kernel,
        out_shape=jax.ShapeDtypeStruct((2 * (UNITS + 1) * tok, 2 * EXPERTS * 8), BF),
        in_specs=[VM, VM, VM],
        out_specs=VM,
        compiler_params=pltpu.CompilerParams(vmem_limit_bytes=16 << 20),
        cost_estimate=pl.CostEstimate(flops=10**8, bytes_accessed=2 * 10**6, transcendentals=0),
        name="gates",
    )(routes_t, tokens, router_t)


def pages_out_kernel(slot_ref, cache_ref, out_ref):
    pages, width = cache_ref.shape
    devices, chunks, _ = out_ref.shape
    chunk = width // chunks
    message = iota((devices, pages), 0)
    first = ((message & 7) * 16 + (message >> 3)) * pages
    slot = slot_ref[...]
    hit = (slot >= first) & (slot < first + pages)
    landing = jnp.sum(jnp.where(hit, slot - first + 1, 0), axis=1, keepdims=True)
    landing = jnp.broadcast_to(landing.astype(F32), (devices, 128))
    pick = onehot(hit)
    for c in range(chunks):
        got = jnp.dot(
            pick, cache_ref[:, c * chunk : (c + 1) * chunk], preferred_element_type=F32
        )
        out_ref[:, c, :chunk] = got.astype(BF)
        out_ref[:, c, chunk:] = landing.astype(BF)


def pages_out(slot_row, cache, devices):
    width = cache.shape[1]
    return pl.pallas_call(
        pages_out_kernel,
        out_shape=jax.ShapeDtypeStruct((devices, CHUNKS, width // CHUNKS + 128), BF),
        in_specs=[VM, VM],
        out_specs=VM,
        compiler_params=pltpu.CompilerParams(vmem_limit_bytes=40 << 20),
        cost_estimate=pl.CostEstimate(flops=2 * 10**9, bytes_accessed=4 * 10**6, transcendentals=0),
        name="pages_out",
    )(slot_row, cache)


def pages_in_kernel(got_ref, out_ref):
    pages, width = out_ref.shape
    devices, chunks, _ = got_ref.shape
    chunk = width // chunks
    landing = got_ref[:, 0, chunk:].astype(F32)
    square = jnp.where(iota((devices, 128), 0) == iota((devices, 128), 1), 1.0, 0.0)
    line = jnp.sum(landing * square, axis=0, keepdims=True).astype(jnp.int32)
    pick = onehot(line == iota((pages, devices), 0) + 1)
    for c in range(chunks):
        placed = jnp.dot(pick, got_ref[:, c, :chunk], preferred_element_type=F32)
        out_ref[:, c * chunk : (c + 1) * chunk] = placed.astype(BF)


def pages_in(got, pages, width):
    return pl.pallas_call(
        pages_in_kernel,
        out_shape=jax.ShapeDtypeStruct((pages, width), BF),
        in_specs=[VM],
        out_specs=VM,
        compiler_params=pltpu.CompilerParams(vmem_limit_bytes=16 << 20),
        cost_estimate=pl.CostEstimate(flops=2 * 10**9, bytes_accessed=4 * 10**6, transcendentals=0),
        name="pages_in",
    )(got)


def experts_kernel(x_ref, w_in_ref, w_out_ref, out_ref):
    rows, packed = x_ref.shape
    unit = packed // UNITS
    hidden = w_out_ref.shape[0]
    block = 128
    row, col = iota((block, UNITS * block), 0), iota((block, UNITS * block), 1)
    sub = row & 7
    inner = col & (block - 1)
    gather = onehot(
        (sub < CAPE)
        & ((row >> 3) == (inner >> 3))
        & ((col >> 7) == (sub >> 1))
        & ((inner & 7) == CAPE + (sub & 1))
    )
    row, col = iota((UNITS * block, block), 0), iota((UNITS * block, block), 1)
    sub = row & 7
    scatter = onehot(
        (sub >= CAPE)
        & (((row & (block - 1)) >> 3) == (col >> 3))
        & ((col & 7) == 2 * (row >> 7) + sub - CAPE)
    )
    tails = []
    for b in range(rows // block):
        part = x_ref[b * block : (b + 1) * block, :]
        part = jnp.concatenate([part[:, u * unit : (u + 1) * unit] for u in range(UNITS)], axis=0)
        tails.append(jnp.dot(gather, part, preferred_element_type=F32).astype(BF))
    tail = jnp.concatenate(tails, axis=0)
    gate_up = jnp.dot(x_ref[...], w_in_ref[: UNITS * unit, :], preferred_element_type=F32)
    gate_up = gate_up + jnp.dot(tail, w_in_ref[UNITS * unit :, :], preferred_element_type=F32)
    act = (jax.nn.silu(gate_up[:, :hidden]) * gate_up[:, hidden:]).astype(BF)
    y = jnp.dot(act, w_out_ref[...], preferred_element_type=F32)
    for b in range(rows // block):
        part = y[b * block : (b + 1) * block, :]
        moved = jnp.dot(scatter, part[:, UNITS * unit :].astype(BF), preferred_element_type=F32)
        keep = (iota((block, unit), 0) & 7) < CAPE
        for u in range(UNITS):
            out_ref[b * block : (b + 1) * block, u * unit : (u + 1) * unit] = jnp.where(
                keep, part[:, u * unit : (u + 1) * unit], moved[u * block : (u + 1) * block, :]
            ).astype(BF)


def experts(x, w_in, w_out):
    rows, packed = x.shape
    step = 256
    once = pl.Buffered(1)
    return pl.pallas_call(
        experts_kernel,
        grid=(rows // step,),
        out_shape=jax.ShapeDtypeStruct(x.shape, BF),
        in_specs=[
            pl.BlockSpec((step, packed), lambda i: (i, 0)),
            pl.BlockSpec(w_in.shape, lambda i: (0, 0), pipeline_mode=once),
            pl.BlockSpec(w_out.shape, lambda i: (0, 0), pipeline_mode=once),
        ],
        out_specs=pl.BlockSpec((step, packed), lambda i: (i, 0)),
        compiler_params=pltpu.CompilerParams(vmem_limit_bytes=40 << 20),
        cost_estimate=pl.CostEstimate(
            flops=10**10, bytes_accessed=15 * 10**6, transcendentals=10**6
        ),
        name="experts",
    )(x, w_in, w_out)


def combine_kernel(gate_hbm, got_ref, out_ref, total_ref, gate_ref, sem):
    tok = out_ref.shape[0]
    unit = got_ref.shape[1] // UNITS
    step = pl.program_id(0)
    steps = gate_ref.shape[0]
    block = gate_ref.shape[2]

    def load(i):
        return pltpu.make_async_copy(
            gate_hbm.at[:, i * block : (i + 1) * block], gate_ref.at[i], sem.at[i]
        )

    @pl.when(step == 0)
    def _():
        for i in range(steps):
            load(i).start()

    for i in range(steps):

        @pl.when(step == i)
        def _():
            load(i).wait()

    gate = gate_ref[step]
    parts = []
    tail = jnp.zeros((2 * tok, unit), F32)
    for u in range(UNITS):
        part = got_ref[:, u * unit : (u + 1) * unit]
        parts.append(jnp.dot(gate[0 : 2 * tok, :], part, preferred_element_type=F32))
        tail = tail + jnp.dot(
            gate[2 * tok * (u + 1) : 2 * tok * (u + 2), :], part, preferred_element_type=F32
        )
    parts.append(tail)

    @pl.when(step == 0)
    def _():
        for u in range(UNITS + 1):
            total_ref[:, u * unit : (u + 1) * unit] = parts[u]

    @pl.when(step > 0)
    def _():
        for u in range(UNITS + 1):
            total_ref[:, u * unit : (u + 1) * unit] += parts[u]

    @pl.when(step == pl.num_programs(0) - 1)
    def _():
        out_ref[...] = (total_ref[:tok, :] + total_ref[tok:, :]).astype(BF)


def combine(gate, got, tok, width):
    rows, packed = got.shape
    step = 256
    return pl.pallas_call(
        combine_kernel,
        grid=(rows // step,),
        out_shape=jax.ShapeDtypeStruct((tok, width), BF),
        in_specs=[
            pl.BlockSpec(memory_space=pltpu.HBM),
            pl.BlockSpec((step, packed), lambda i: (i, 0)),
        ],
        out_specs=pl.BlockSpec((tok, width), lambda i: (0, 0)),
        scratch_shapes=[
            pltpu.VMEM((2 * tok, width), F32),
            pltpu.VMEM((rows // step, gate.shape[0], step), BF),
            pltpu.SemaphoreType.DMA((rows // step,)),
        ],
        compiler_params=pltpu.CompilerParams(vmem_limit_bytes=12 << 20),
        cost_estimate=pl.CostEstimate(flops=10**9, bytes_accessed=4 * 10**6, transcendentals=0),
        name="combine",
    )(gate, got)


def swap(x):
    return lax.all_to_all(x, SWAP, split_axis=0, concat_axis=0, tiled=True)


def per_device(tokens, routes, router, w_in, w_out, cache_prefill, page_slot):
    devices = lax.axis_size("row") * lax.axis_size("col")
    pages = page_slot.shape[0]
    routes_t = routes.T
    arrived = swap(dispatch(routes_t, tokens))
    gate = gates(routes_t, tokens, router.T)
    moved = swap(pages_out(page_slot.reshape(1, pages), cache_prefill, devices))
    returned = swap(experts(arrived, w_in[0], w_out[0]))
    cache_decode = pages_in(moved, pages, cache_prefill.shape[1])
    moe_out = combine(gate, returned, tokens.shape[0], tokens.shape[1])
    return (moe_out, cache_decode)


def solution(mesh):
    in_specs = (
        P(AXES, None),
        P(AXES, None),
        P(),
        P(AXES, None, None),
        P(AXES, None, None),
        P(AXES, None),
        P(AXES),
    )
    out_specs = (P(AXES, None), P(AXES, None))
    return jax.shard_map(
        per_device, mesh=mesh, in_specs=in_specs, out_specs=out_specs, check_vma=False
    )
```

```python
import functools

import jax
import jax.numpy as jnp
from jax import lax
from jax.experimental import pallas as pl
from jax.experimental.pallas import tpu as pltpu
from jax.sharding import PartitionSpec as P

EXPERTS = 64
CAPE = 6
CHUNKS = 2
ROUTE_SCALE = 2.446
AXES = ("row", "col")
SWAP = ("col", "row")
BF = jnp.bfloat16
F32 = jnp.float32
VM = pl.BlockSpec(memory_space=pltpu.VMEM)


UNITS = 3


def iota(shape, dim):
    return lax.broadcasted_iota(jnp.int32, shape, dim)


def onehot(cond):
    return jnp.where(cond, 1.0, 0.0).astype(BF)


def expert_of(message):
    return ((message & 3) << 4) + (message >> 3)


def dispatch_kernel(routes_hbm, tok_hbm, out_hbm, routes_ref, tok_ref, buf_ref, in_sem, out_sem):
    tok = tok_ref.shape[0]
    rows = EXPERTS * 8
    unit = buf_ref.shape[3]
    load_routes = pltpu.make_async_copy(routes_hbm, routes_ref, in_sem.at[0])
    load_tok = pltpu.make_async_copy(tok_hbm, tok_ref, in_sem.at[1])
    load_routes.start()
    load_tok.start()
    load_routes.wait()
    row, col = iota((rows, 2 * tok), 0), iota((rows, 2 * tok), 1)
    expert, sub = expert_of(((row >> 5) << 3) + ((row >> 3) & 3)), row & 7
    routes = jnp.concatenate([routes_ref[...], routes_ref[...]], axis=1)
    named = routes[0:1, :] == expert
    for k in range(1, routes_ref.shape[0]):
        named = named | (routes[k : k + 1, :] == expert)
    first, second = iota((2 * tok, 2 * tok), 0), iota((2 * tok, 2 * tok), 1)
    before = onehot(first < jnp.where(second < tok, second, second - tok))
    rank = jnp.dot(onehot(named), before, preferred_element_type=F32).astype(jnp.int32)
    rank = jnp.where(named, rank, 99)
    load_tok.wait()
    last = tok_ref[:, UNITS * unit :]
    stores = []
    for u in range(UNITS):
        wanted = jnp.where(col < tok, sub, jnp.where(sub >= CAPE, sub + (2 * u - CAPE), -1))
        source = jnp.concatenate([tok_ref[:, u * unit : (u + 1) * unit], last], axis=0)
        picked = jnp.dot(onehot(rank == wanted), source, preferred_element_type=F32)
        buf_ref[u] = picked.astype(BF).reshape(buf_ref.shape[1:])
        for half in range(2):
            store = pltpu.make_async_copy(
                buf_ref.at[u],
                out_hbm.at[:, half, :, u * unit : (u + 1) * unit],
                out_sem.at[2 * u + half],
            )
            store.start()
            stores.append(store)
    for store in stores:
        store.wait()


def dispatch(routes_t, tokens):
    width = tokens.shape[1]
    unit = width * CAPE // 8 // UNITS
    hbm = pl.BlockSpec(memory_space=pltpu.HBM)
    out = pl.pallas_call(
        dispatch_kernel,
        out_shape=jax.ShapeDtypeStruct((16, 2, 32, UNITS * unit), BF),
        in_specs=[hbm, hbm],
        out_specs=hbm,
        scratch_shapes=[
            pltpu.VMEM(routes_t.shape, jnp.int32),
            pltpu.VMEM(tokens.shape, BF),
            pltpu.VMEM((UNITS, 16, 32, unit), BF),
            pltpu.SemaphoreType.DMA((2,)),
            pltpu.SemaphoreType.DMA((2 * UNITS,)),
        ],
        cost_estimate=pl.CostEstimate(flops=10**8, bytes_accessed=4 * 10**6, transcendentals=0),
        name="dispatch",
    )(routes_t, tokens)
    return out.reshape(2 * EXPERTS * 8, UNITS * unit)


def gates_kernel(routes_ref, tok_ref, router_ref, out_ref):
    tok = tok_ref.shape[0]
    cols = out_ref.shape[1]
    logits = lax.dot_general(
        tok_ref[...], router_ref[...], (((1,), (1,)), ((), ())), preferred_element_type=F32
    )
    scores = jax.nn.sigmoid(logits)
    expert = iota((EXPERTS, tok), 0)
    named = routes_ref[0:1, :] == expert
    for k in range(1, routes_ref.shape[0]):
        named = named | (routes_ref[k : k + 1, :] == expert)
    unit = onehot(iota((tok, tok), 0) == iota((tok, tok), 1))
    mine = lax.dot_general(
        unit, onehot(named), (((1,), (1,)), ((), ())), preferred_element_type=F32
    )
    before = onehot(iota((tok, tok), 1) < iota((tok, tok), 0))
    rank = jnp.dot(before, mine.astype(BF), preferred_element_type=F32)
    rank = jnp.where(mine > 0.5, rank, 99.0)
    picked = jnp.where(mine > 0.5, scores, 0.0)
    gate = ROUTE_SCALE * picked / jnp.sum(picked, axis=1, keepdims=True)
    high = gate.astype(BF)
    low = (gate - high.astype(F32)).astype(BF)
    spread = onehot(expert_of(iota((EXPERTS, cols), 1) >> 3) == iota((EXPERTS, cols), 0))
    rank = jnp.dot(rank.astype(BF), spread, preferred_element_type=F32).astype(jnp.int32)
    high = jnp.dot(high, spread, preferred_element_type=F32)
    low = jnp.dot(low, spread, preferred_element_type=F32)
    sub = iota((tok, cols), 1) & 7
    for u in range(UNITS + 1):
        if u == 0:
            keep = rank == sub
        else:
            keep = (sub >= CAPE) & (rank == sub + (2 * (u - 1) - CAPE))
        out_ref[2 * u * tok : (2 * u + 1) * tok, :] = jnp.where(keep, high, 0.0).astype(BF)
        out_ref[(2 * u + 1) * tok : (2 * u + 2) * tok, :] = jnp.where(keep, low, 0.0).astype(BF)


def gates(routes_t, tokens, router_t):
    tok = tokens.shape[0]
    return pl.pallas_call(
        gates_kernel,
        out_shape=jax.ShapeDtypeStruct((2 * (UNITS + 1) * tok, 2 * EXPERTS * 8), BF),
        in_specs=[VM, VM, VM],
        out_specs=VM,
        compiler_params=pltpu.CompilerParams(vmem_limit_bytes=16 << 20),
        cost_estimate=pl.CostEstimate(flops=10**8, bytes_accessed=2 * 10**6, transcendentals=0),
        name="gates",
    )(routes_t, tokens, router_t)


def pages_out_kernel(slot_ref, cache_ref, out_ref):
    pages, width = cache_ref.shape
    devices, chunks, _ = out_ref.shape
    chunk = width // chunks
    message = iota((devices, pages), 0)
    first = ((message & 7) * 16 + (message >> 3)) * pages
    slot = slot_ref[...]
    hit = (slot >= first) & (slot < first + pages)
    landing = jnp.sum(jnp.where(hit, slot - first + 1, 0), axis=1, keepdims=True)
    landing = jnp.broadcast_to(landing.astype(F32), (devices, 128))
    pick = onehot(hit)
    for c in range(chunks):
        got = jnp.dot(
            pick, cache_ref[:, c * chunk : (c + 1) * chunk], preferred_element_type=F32
        )
        out_ref[:, c, :chunk] = got.astype(BF)
        out_ref[:, c, chunk:] = landing.astype(BF)


def pages_out(slot_row, cache, devices):
    width = cache.shape[1]
    return pl.pallas_call(
        pages_out_kernel,
        out_shape=jax.ShapeDtypeStruct((devices, CHUNKS, width // CHUNKS + 128), BF),
        in_specs=[VM, VM],
        out_specs=VM,
        compiler_params=pltpu.CompilerParams(vmem_limit_bytes=40 << 20),
        cost_estimate=pl.CostEstimate(flops=2 * 10**9, bytes_accessed=4 * 10**6, transcendentals=0),
        name="pages_out",
    )(slot_row, cache)


def pages_in_kernel(got_ref, out_ref):
    pages, width = out_ref.shape
    devices, chunks, _ = got_ref.shape
    chunk = width // chunks
    landing = got_ref[:, 0, chunk:].astype(F32)
    square = jnp.where(iota((devices, 128), 0) == iota((devices, 128), 1), 1.0, 0.0)
    line = jnp.sum(landing * square, axis=0, keepdims=True).astype(jnp.int32)
    pick = onehot(line == iota((pages, devices), 0) + 1)
    for c in range(chunks):
        placed = jnp.dot(pick, got_ref[:, c, :chunk], preferred_element_type=F32)
        out_ref[:, c * chunk : (c + 1) * chunk] = placed.astype(BF)


def pages_in(got, pages, width):
    return pl.pallas_call(
        pages_in_kernel,
        out_shape=jax.ShapeDtypeStruct((pages, width), BF),
        in_specs=[VM],
        out_specs=VM,
        compiler_params=pltpu.CompilerParams(vmem_limit_bytes=16 << 20),
        cost_estimate=pl.CostEstimate(flops=2 * 10**9, bytes_accessed=4 * 10**6, transcendentals=0),
        name="pages_in",
    )(got)


def experts_kernel(x_ref, w_in_ref, w_out_ref, out_ref):
    rows, packed = x_ref.shape
    unit = packed // UNITS
    hidden = w_out_ref.shape[0]
    block = 128
    row, col = iota((block, UNITS * block), 0), iota((block, UNITS * block), 1)
    sub = row & 7
    inner = col & (block - 1)
    gather = onehot(
        (sub < CAPE)
        & ((row >> 3) == (inner >> 3))
        & ((col >> 7) == (sub >> 1))
        & ((inner & 7) == CAPE + (sub & 1))
    )
    row, col = iota((UNITS * block, block), 0), iota((UNITS * block, block), 1)
    sub = row & 7
    scatter = onehot(
        (sub >= CAPE)
        & (((row & (block - 1)) >> 3) == (col >> 3))
        & ((col & 7) == 2 * (row >> 7) + sub - CAPE)
    )
    tails = []
    for b in range(rows // block):
        part = x_ref[b * block : (b + 1) * block, :]
        part = jnp.concatenate([part[:, u * unit : (u + 1) * unit] for u in range(UNITS)], axis=0)
        tails.append(jnp.dot(gather, part, preferred_element_type=F32).astype(BF))
    tail = jnp.concatenate(tails, axis=0)
    gate_up = jnp.dot(x_ref[...], w_in_ref[: UNITS * unit, :], preferred_element_type=F32)
    gate_up = gate_up + jnp.dot(tail, w_in_ref[UNITS * unit :, :], preferred_element_type=F32)
    act = (jax.nn.silu(gate_up[:, :hidden]) * gate_up[:, hidden:]).astype(BF)
    y = jnp.dot(act, w_out_ref[...], preferred_element_type=F32)
    for b in range(rows // block):
        part = y[b * block : (b + 1) * block, :]
        moved = jnp.dot(scatter, part[:, UNITS * unit :].astype(BF), preferred_element_type=F32)
        keep = (iota((block, unit), 0) & 7) < CAPE
        for u in range(UNITS):
            out_ref[b * block : (b + 1) * block, u * unit : (u + 1) * unit] = jnp.where(
                keep, part[:, u * unit : (u + 1) * unit], moved[u * block : (u + 1) * block, :]
            ).astype(BF)


def experts(x, w_in, w_out):
    rows, packed = x.shape
    step = 256
    once = pl.Buffered(1)
    return pl.pallas_call(
        experts_kernel,
        grid=(rows // step,),
        out_shape=jax.ShapeDtypeStruct(x.shape, BF),
        in_specs=[
            pl.BlockSpec((step, packed), lambda i: (i, 0)),
            pl.BlockSpec(w_in.shape, lambda i: (0, 0), pipeline_mode=once),
            pl.BlockSpec(w_out.shape, lambda i: (0, 0), pipeline_mode=once),
        ],
        out_specs=pl.BlockSpec((step, packed), lambda i: (i, 0)),
        compiler_params=pltpu.CompilerParams(vmem_limit_bytes=40 << 20),
        cost_estimate=pl.CostEstimate(
            flops=10**10, bytes_accessed=15 * 10**6, transcendentals=10**6
        ),
        name="experts",
    )(x, w_in, w_out)


def combine_kernel(gate_hbm, got_ref, out_ref, gate_ref, sem):
    tok = out_ref.shape[0]
    unit = got_ref.shape[1] // UNITS
    blocks, _, block = gate_ref.shape
    loads = []
    for i in range(blocks):
        load = pltpu.make_async_copy(
            gate_hbm.at[:, i * block : (i + 1) * block], gate_ref.at[i], sem.at[i]
        )
        load.start()
        loads.append(load)
    total = [jnp.zeros((2 * tok, unit), F32) for _ in range(UNITS + 1)]
    for i in range(blocks):
        loads[i].wait()
        for u in range(UNITS):
            part = got_ref[i * block : (i + 1) * block, u * unit : (u + 1) * unit]
            main = gate_ref[i, 0 : 2 * tok, :]
            tail = gate_ref[i, 2 * tok * (u + 1) : 2 * tok * (u + 2), :]
            both = jnp.dot(
                jnp.concatenate([main, tail], axis=0), part, preferred_element_type=F32
            )
            total[u] = total[u] + both[: 2 * tok]
            total[UNITS] = total[UNITS] + both[2 * tok :]
    for u in range(UNITS + 1):
        out_ref[:, u * unit : (u + 1) * unit] = (total[u][:tok] + total[u][tok:]).astype(BF)


def combine(gate, got, tok, width):
    rows = got.shape[0]
    block = 256
    return pl.pallas_call(
        combine_kernel,
        out_shape=jax.ShapeDtypeStruct((tok, width), BF),
        in_specs=[pl.BlockSpec(memory_space=pltpu.HBM), VM],
        out_specs=VM,
        scratch_shapes=[
            pltpu.VMEM((rows // block, gate.shape[0], block), BF),
            pltpu.SemaphoreType.DMA((rows // block,)),
        ],
        compiler_params=pltpu.CompilerParams(vmem_limit_bytes=12 << 20),
        cost_estimate=pl.CostEstimate(flops=10**9, bytes_accessed=4 * 10**6, transcendentals=0),
        name="combine",
    )(pltpu.with_memory_space_constraint(gate, pltpu.HBM), got)


def swap(x):
    return lax.all_to_all(x, SWAP, split_axis=0, concat_axis=0, tiled=True)


def per_device(tokens, routes, router, w_in, w_out, cache_prefill, page_slot):
    devices = lax.axis_size("row") * lax.axis_size("col")
    pages = page_slot.shape[0]
    routes_t = routes.T
    arrived = swap(dispatch(routes_t, tokens))
    gate = gates(routes_t, tokens, router.T)
    moved = swap(pages_out(page_slot.reshape(1, pages), cache_prefill, devices))
    returned = swap(experts(arrived, w_in[0], w_out[0]))
    cache_decode = pages_in(moved, pages, cache_prefill.shape[1])
    moe_out = combine(gate, returned, tokens.shape[0], tokens.shape[1])
    return (moe_out, cache_decode)


def solution(mesh):
    in_specs = (
        P(AXES, None),
        P(AXES, None),
        P(),
        P(AXES, None, None),
        P(AXES, None, None),
        P(AXES, None),
        P(AXES),
    )
    out_specs = (P(AXES, None), P(AXES, None))
    return jax.shard_map(
        per_device, mesh=mesh, in_specs=in_specs, out_specs=out_specs, check_vma=False
    )
```

```python
import functools

import jax
import jax.numpy as jnp
from jax import lax
from jax.experimental import pallas as pl
from jax.experimental.pallas import tpu as pltpu
from jax.sharding import PartitionSpec as P

EXPERTS = 64
CAPE = 6
CHUNKS = 2
ROUTE_SCALE = 2.446
AXES = ("row", "col")
SWAP = ("col", "row")
BF = jnp.bfloat16
F32 = jnp.float32
VM = pl.BlockSpec(memory_space=pltpu.VMEM)


UNITS = 3


def iota(shape, dim):
    return lax.broadcasted_iota(jnp.int32, shape, dim)


def onehot(cond):
    return jnp.where(cond, 1.0, 0.0).astype(BF)


def slot_expert(row):
    return (((row >> 3) & 3) << 4) + (row >> 5)


def dispatch_kernel(routes_hbm, tok_hbm, out_hbm, routes_ref, tok_ref, buf_ref, in_sem, out_sem):
    tok = tok_ref.shape[0]
    rows = EXPERTS * 8
    unit = buf_ref.shape[3]
    load_routes = pltpu.make_async_copy(routes_hbm, routes_ref, in_sem.at[0])
    load_tok = pltpu.make_async_copy(tok_hbm, tok_ref, in_sem.at[1])
    load_routes.start()
    load_tok.start()
    load_routes.wait()
    row, col = iota((rows, 2 * tok), 0), iota((rows, 2 * tok), 1)
    expert, sub = slot_expert(row), row & 7
    routes = jnp.concatenate([routes_ref[...], routes_ref[...]], axis=1)
    named = routes[0:1, :] == expert
    for k in range(1, routes_ref.shape[0]):
        named = named | (routes[k : k + 1, :] == expert)
    first, second = iota((2 * tok, 2 * tok), 0), iota((2 * tok, 2 * tok), 1)
    before = onehot(first < jnp.where(second < tok, second, second - tok))
    rank = jnp.dot(onehot(named), before, preferred_element_type=F32).astype(jnp.int32)
    rank = jnp.where(named, rank, 99)
    load_tok.wait()
    last = tok_ref[:, UNITS * unit :]
    stores = []
    for u in range(UNITS):
        wanted = jnp.where(col < tok, sub, jnp.where(sub >= CAPE, sub + (2 * u - CAPE), -1))
        source = jnp.concatenate([tok_ref[:, u * unit : (u + 1) * unit], last], axis=0)
        picked = jnp.dot(onehot(rank == wanted), source, preferred_element_type=F32)
        buf_ref[u] = picked.astype(BF).reshape(buf_ref.shape[1:])
        for half in range(2):
            store = pltpu.make_async_copy(
                buf_ref.at[u],
                out_hbm.at[:, half, :, u * unit : (u + 1) * unit],
                out_sem.at[2 * u + half],
            )
            store.start()
            stores.append(store)
    for store in stores:
        store.wait()


def dispatch(routes_t, tokens):
    width = tokens.shape[1]
    unit = width * CAPE // 8 // UNITS
    hbm = pl.BlockSpec(memory_space=pltpu.HBM)
    out = pl.pallas_call(
        dispatch_kernel,
        out_shape=jax.ShapeDtypeStruct((16, 2, 32, UNITS * unit), BF),
        in_specs=[hbm, hbm],
        out_specs=hbm,
        scratch_shapes=[
            pltpu.VMEM(routes_t.shape, jnp.int32),
            pltpu.VMEM(tokens.shape, BF),
            pltpu.VMEM((UNITS, 16, 32, unit), BF),
            pltpu.SemaphoreType.DMA((2,)),
            pltpu.SemaphoreType.DMA((2 * UNITS,)),
        ],
        cost_estimate=pl.CostEstimate(flops=10**8, bytes_accessed=4 * 10**6, transcendentals=0),
        name="dispatch",
    )(routes_t, tokens)
    return out.reshape(2 * EXPERTS * 8, UNITS * unit)


def gates_kernel(routes_ref, tok_ref, router_ref, out_ref):
    tok = tok_ref.shape[0]
    cols = out_ref.shape[1]
    logits = lax.dot_general(
        tok_ref[...], router_ref[...], (((1,), (1,)), ((), ())), preferred_element_type=F32
    )
    scores = jax.nn.sigmoid(logits)
    expert = iota((EXPERTS, tok), 0)
    named = routes_ref[0:1, :] == expert
    for k in range(1, routes_ref.shape[0]):
        named = named | (routes_ref[k : k + 1, :] == expert)
    unit = onehot(iota((tok, tok), 0) == iota((tok, tok), 1))
    mine = lax.dot_general(
        unit, onehot(named), (((1,), (1,)), ((), ())), preferred_element_type=F32
    )
    before = onehot(iota((tok, tok), 1) < iota((tok, tok), 0))
    rank = jnp.dot(before, mine.astype(BF), preferred_element_type=F32)
    rank = jnp.where(mine > 0.5, rank, 99.0)
    picked = jnp.where(mine > 0.5, scores, 0.0)
    gate = ROUTE_SCALE * picked / jnp.sum(picked, axis=1, keepdims=True)
    high = gate.astype(BF)
    low = (gate - high.astype(F32)).astype(BF)
    spread = onehot(slot_expert(iota((EXPERTS, cols), 1)) == iota((EXPERTS, cols), 0))
    rank = jnp.dot(rank.astype(BF), spread, preferred_element_type=F32).astype(jnp.int32)
    high = jnp.dot(high, spread, preferred_element_type=F32)
    low = jnp.dot(low, spread, preferred_element_type=F32)
    sub = iota((tok, cols), 1) & 7
    for u in range(UNITS + 1):
        if u == 0:
            keep = rank == sub
        else:
            keep = (sub >= CAPE) & (rank == sub + (2 * (u - 1) - CAPE))
        out_ref[2 * u * tok : (2 * u + 1) * tok, :] = jnp.where(keep, high, 0.0).astype(BF)
        out_ref[(2 * u + 1) * tok : (2 * u + 2) * tok, :] = jnp.where(keep, low, 0.0).astype(BF)


def gates(routes_t, tokens, router_t):
    tok = tokens.shape[0]
    return pl.pallas_call(
        gates_kernel,
        out_shape=jax.ShapeDtypeStruct((2 * (UNITS + 1) * tok, EXPERTS * 8), BF),
        in_specs=[VM, VM, VM],
        out_specs=VM,
        compiler_params=pltpu.CompilerParams(vmem_limit_bytes=16 << 20),
        cost_estimate=pl.CostEstimate(flops=10**8, bytes_accessed=2 * 10**6, transcendentals=0),
        name="gates",
    )(routes_t, tokens, router_t)


def pages_out_kernel(slot_ref, cache_ref, out_ref):
    pages, width = cache_ref.shape
    devices, chunks, _ = out_ref.shape
    chunk = width // chunks
    message = iota((devices, pages), 0)
    first = ((message & 7) * 16 + (message >> 3)) * pages
    slot = slot_ref[...]
    hit = (slot >= first) & (slot < first + pages)
    landing = jnp.sum(jnp.where(hit, slot - first + 1, 0), axis=1, keepdims=True)
    landing = jnp.broadcast_to(landing.astype(F32), (devices, 128))
    pick = onehot(hit)
    for c in range(chunks):
        got = jnp.dot(
            pick, cache_ref[:, c * chunk : (c + 1) * chunk], preferred_element_type=F32
        )
        out_ref[:, c, :chunk] = got.astype(BF)
        out_ref[:, c, chunk:] = landing.astype(BF)


def pages_out(slot_row, cache, devices):
    width = cache.shape[1]
    return pl.pallas_call(
        pages_out_kernel,
        out_shape=jax.ShapeDtypeStruct((devices, CHUNKS, width // CHUNKS + 128), BF),
        in_specs=[VM, VM],
        out_specs=VM,
        compiler_params=pltpu.CompilerParams(vmem_limit_bytes=40 << 20),
        cost_estimate=pl.CostEstimate(flops=2 * 10**9, bytes_accessed=4 * 10**6, transcendentals=0),
        name="pages_out",
    )(slot_row, cache)


def pages_in_kernel(got_ref, out_ref):
    pages, width = out_ref.shape
    devices, chunks, _ = got_ref.shape
    chunk = width // chunks
    landing = got_ref[:, 0, chunk:].astype(F32)
    square = jnp.where(iota((devices, 128), 0) == iota((devices, 128), 1), 1.0, 0.0)
    line = jnp.sum(landing * square, axis=0, keepdims=True).astype(jnp.int32)
    pick = onehot(line == iota((pages, devices), 0) + 1)
    for c in range(chunks):
        placed = jnp.dot(pick, got_ref[:, c, :chunk], preferred_element_type=F32)
        out_ref[:, c * chunk : (c + 1) * chunk] = placed.astype(BF)


def pages_in(got, pages, width):
    return pl.pallas_call(
        pages_in_kernel,
        out_shape=jax.ShapeDtypeStruct((pages, width), BF),
        in_specs=[VM],
        out_specs=VM,
        compiler_params=pltpu.CompilerParams(vmem_limit_bytes=16 << 20),
        cost_estimate=pl.CostEstimate(flops=2 * 10**9, bytes_accessed=4 * 10**6, transcendentals=0),
        name="pages_in",
    )(got)


def experts_kernel(x_ref, w_in_ref, w_out_ref, out_ref):
    rows, packed = x_ref.shape
    unit = packed // UNITS
    hidden = w_out_ref.shape[0]
    block = 128
    row, col = iota((block, UNITS * block), 0), iota((block, UNITS * block), 1)
    sub = row & 7
    inner = col & (block - 1)
    gather = onehot(
        (sub < CAPE)
        & ((row >> 3) == (inner >> 3))
        & ((col >> 7) == (sub >> 1))
        & ((inner & 7) == CAPE + (sub & 1))
    )
    row, col = iota((UNITS * block, block), 0), iota((UNITS * block, block), 1)
    sub = row & 7
    scatter = onehot(
        (sub >= CAPE)
        & (((row & (block - 1)) >> 3) == (col >> 3))
        & ((col & 7) == 2 * (row >> 7) + sub - CAPE)
    )
    tails = []
    for b in range(rows // block):
        part = x_ref[b * block : (b + 1) * block, :]
        part = jnp.concatenate([part[:, u * unit : (u + 1) * unit] for u in range(UNITS)], axis=0)
        tails.append(jnp.dot(gather, part, preferred_element_type=F32).astype(BF))
    tail = jnp.concatenate(tails, axis=0)
    gate_up = jnp.dot(x_ref[...], w_in_ref[: UNITS * unit, :], preferred_element_type=F32)
    gate_up = gate_up + jnp.dot(tail, w_in_ref[UNITS * unit :, :], preferred_element_type=F32)
    act = (jax.nn.silu(gate_up[:, :hidden]) * gate_up[:, hidden:]).astype(BF)
    y = jnp.dot(act, w_out_ref[...], preferred_element_type=F32)
    for b in range(rows // block):
        part = y[b * block : (b + 1) * block, :]
        moved = jnp.dot(scatter, part[:, UNITS * unit :].astype(BF), preferred_element_type=F32)
        keep = (iota((block, unit), 0) & 7) < CAPE
        for u in range(UNITS):
            out_ref[b * block : (b + 1) * block, u * unit : (u + 1) * unit] = jnp.where(
                keep, part[:, u * unit : (u + 1) * unit], moved[u * block : (u + 1) * block, :]
            ).astype(BF)


def experts(x, w_in, w_out):
    rows, packed = x.shape
    step = 256
    once = pl.Buffered(1)
    return pl.pallas_call(
        experts_kernel,
        grid=(rows // step,),
        out_shape=jax.ShapeDtypeStruct(x.shape, BF),
        in_specs=[
            pl.BlockSpec((step, packed), lambda i: (i, 0)),
            pl.BlockSpec(w_in.shape, lambda i: (0, 0), pipeline_mode=once),
            pl.BlockSpec(w_out.shape, lambda i: (0, 0), pipeline_mode=once),
        ],
        out_specs=pl.BlockSpec((step, packed), lambda i: (i, 0)),
        compiler_params=pltpu.CompilerParams(vmem_limit_bytes=40 << 20),
        cost_estimate=pl.CostEstimate(
            flops=10**10, bytes_accessed=15 * 10**6, transcendentals=10**6
        ),
        name="experts",
    )(x, w_in, w_out)


def combine_kernel(gate_hbm, got_ref, out_ref, sum_ref, gate_ref, sem):
    tok = out_ref.shape[0]
    unit = got_ref.shape[2] // UNITS
    load = pltpu.make_async_copy(gate_hbm, gate_ref, sem)
    load.start()
    sums = got_ref[:, :32, :].astype(F32) + got_ref[:, 32:, :].astype(F32)
    sum_ref[...] = sums.astype(BF).reshape(sum_ref.shape)
    load.wait()
    main = gate_ref[0 : 2 * tok, :]
    total = jnp.zeros((2 * tok, unit), F32)
    for u in range(UNITS):
        tail = gate_ref[2 * tok * (u + 1) : 2 * tok * (u + 2), :]
        both = jnp.dot(
            jnp.concatenate([main, tail], axis=0),
            sum_ref[:, u * unit : (u + 1) * unit],
            preferred_element_type=F32,
        )
        out_ref[:, u * unit : (u + 1) * unit] = (both[:tok] + both[tok : 2 * tok]).astype(BF)
        total = total + both[2 * tok :]
    out_ref[:, UNITS * unit :] = (total[:tok] + total[tok:]).astype(BF)


def combine(gate, got, tok, width):
    rows, packed = got.shape
    return pl.pallas_call(
        combine_kernel,
        out_shape=jax.ShapeDtypeStruct((tok, width), BF),
        in_specs=[pl.BlockSpec(memory_space=pltpu.HBM), VM],
        out_specs=VM,
        scratch_shapes=[
            pltpu.VMEM((rows // 2, packed), BF),
            pltpu.VMEM(gate.shape, BF),
            pltpu.SemaphoreType.DMA,
        ],
        compiler_params=pltpu.CompilerParams(vmem_limit_bytes=12 << 20),
        cost_estimate=pl.CostEstimate(flops=10**9, bytes_accessed=4 * 10**6, transcendentals=0),
        name="combine",
    )(pltpu.with_memory_space_constraint(gate, pltpu.HBM), got.reshape(16, 64, packed))


def swap(x):
    return lax.all_to_all(x, SWAP, split_axis=0, concat_axis=0, tiled=True)


def per_device(tokens, routes, router, w_in, w_out, cache_prefill, page_slot):
    devices = lax.axis_size("row") * lax.axis_size("col")
    pages = page_slot.shape[0]
    routes_t = routes.T
    arrived = swap(dispatch(routes_t, tokens))
    gate = gates(routes_t, tokens, router.T)
    moved = swap(pages_out(page_slot.reshape(1, pages), cache_prefill, devices))
    returned = swap(experts(arrived, w_in[0], w_out[0]))
    cache_decode = pages_in(moved, pages, cache_prefill.shape[1])
    moe_out = combine(gate, returned, tokens.shape[0], tokens.shape[1])
    return (moe_out, cache_decode)


def solution(mesh):
    in_specs = (
        P(AXES, None),
        P(AXES, None),
        P(),
        P(AXES, None, None),
        P(AXES, None, None),
        P(AXES, None),
        P(AXES),
    )
    out_specs = (P(AXES, None), P(AXES, None))
    return jax.shard_map(
        per_device, mesh=mesh, in_specs=in_specs, out_specs=out_specs, check_vma=False
    )
```

```python
import functools

import jax
import jax.numpy as jnp
from jax import lax
from jax.experimental import pallas as pl
from jax.experimental.pallas import tpu as pltpu
from jax.sharding import PartitionSpec as P

EXPERTS = 64
CAPE = 6
CHUNKS = 2
ROUTE_SCALE = 2.446
AXES = ("row", "col")
SWAP = ("col", "row")
BF = jnp.bfloat16
F32 = jnp.float32
VM = pl.BlockSpec(memory_space=pltpu.VMEM)


UNITS = 3


def iota(shape, dim):
    return lax.broadcasted_iota(jnp.int32, shape, dim)


def onehot(cond):
    return jnp.where(cond, 1.0, 0.0).astype(BF)


def slot_expert(row):
    return (((row >> 3) & 3) << 4) + (row >> 5)


def dispatch_kernel(routes_hbm, tok_hbm, out_hbm, routes_ref, tok_ref, buf_ref, in_sem, out_sem):
    tok = tok_ref.shape[0]
    rows = EXPERTS * 8
    unit = buf_ref.shape[3]
    load_routes = pltpu.make_async_copy(routes_hbm, routes_ref, in_sem.at[0])
    load_tok = pltpu.make_async_copy(tok_hbm, tok_ref, in_sem.at[1])
    load_routes.start()
    load_tok.start()
    load_routes.wait()
    row, col = iota((rows, 2 * tok), 0), iota((rows, 2 * tok), 1)
    expert, sub = slot_expert(row), row & 7
    routes = jnp.concatenate([routes_ref[...], routes_ref[...]], axis=1)
    named = routes[0:1, :] == expert
    for k in range(1, routes_ref.shape[0]):
        named = named | (routes[k : k + 1, :] == expert)
    first, second = iota((2 * tok, 2 * tok), 0), iota((2 * tok, 2 * tok), 1)
    before = onehot(first < jnp.where(second < tok, second, second - tok))
    rank = jnp.dot(onehot(named), before, preferred_element_type=F32).astype(jnp.int32)
    rank = jnp.where(named, rank, 99)
    load_tok.wait()
    last = tok_ref[:, UNITS * unit :]
    stores = []
    for u in range(UNITS):
        wanted = jnp.where(col < tok, sub, jnp.where(sub >= CAPE, sub + (2 * u - CAPE), -1))
        source = jnp.concatenate([tok_ref[:, u * unit : (u + 1) * unit], last], axis=0)
        picked = jnp.dot(onehot(rank == wanted), source, preferred_element_type=F32)
        buf_ref[u] = picked.astype(BF).reshape(buf_ref.shape[1:])
        for half in range(2):
            store = pltpu.make_async_copy(
                buf_ref.at[u],
                out_hbm.at[:, half, :, u * unit : (u + 1) * unit],
                out_sem.at[2 * u + half],
            )
            store.start()
            stores.append(store)
    for store in stores:
        store.wait()


def dispatch(routes_t, tokens):
    width = tokens.shape[1]
    unit = width * CAPE // 8 // UNITS
    hbm = pl.BlockSpec(memory_space=pltpu.HBM)
    out = pl.pallas_call(
        dispatch_kernel,
        out_shape=jax.ShapeDtypeStruct((16, 2, 32, UNITS * unit), BF),
        in_specs=[hbm, hbm],
        out_specs=hbm,
        scratch_shapes=[
            pltpu.VMEM(routes_t.shape, jnp.int32),
            pltpu.VMEM(tokens.shape, BF),
            pltpu.VMEM((UNITS, 16, 32, unit), BF),
            pltpu.SemaphoreType.DMA((2,)),
            pltpu.SemaphoreType.DMA((2 * UNITS,)),
        ],
        cost_estimate=pl.CostEstimate(flops=10**8, bytes_accessed=4 * 10**6, transcendentals=0),
        name="dispatch",
    )(routes_t, tokens)
    return out.reshape(2 * EXPERTS * 8, UNITS * unit)


def gates_kernel(routes_ref, tok_ref, router_ref, out_ref):
    tok = tok_ref.shape[0]
    cols = out_ref.shape[1]
    logits = lax.dot_general(
        tok_ref[...], router_ref[...], (((1,), (1,)), ((), ())), preferred_element_type=F32
    )
    scores = jax.nn.sigmoid(logits)
    expert = iota((EXPERTS, tok), 0)
    named = routes_ref[0:1, :] == expert
    for k in range(1, routes_ref.shape[0]):
        named = named | (routes_ref[k : k + 1, :] == expert)
    unit = onehot(iota((tok, tok), 0) == iota((tok, tok), 1))
    mine = lax.dot_general(
        unit, onehot(named), (((1,), (1,)), ((), ())), preferred_element_type=F32
    )
    before = onehot(iota((tok, tok), 1) < iota((tok, tok), 0))
    rank = jnp.dot(before, mine.astype(BF), preferred_element_type=F32)
    rank = jnp.where(mine > 0.5, rank, 99.0)
    picked = jnp.where(mine > 0.5, scores, 0.0)
    gate = ROUTE_SCALE * picked / jnp.sum(picked, axis=1, keepdims=True)
    high = gate.astype(BF)
    low = (gate - high.astype(F32)).astype(BF)
    spread = onehot(slot_expert(iota((EXPERTS, cols), 1)) == iota((EXPERTS, cols), 0))
    rank = jnp.dot(rank.astype(BF), spread, preferred_element_type=F32).astype(jnp.int32)
    high = jnp.dot(high, spread, preferred_element_type=F32)
    low = jnp.dot(low, spread, preferred_element_type=F32)
    sub = iota((tok, cols), 1) & 7
    for u in range(UNITS):
        keep = (sub >= CAPE) & (rank == sub + (2 * u - CAPE))
        if u == 0:
            keep = keep | (rank == sub)
        out_ref[2 * u * tok : (2 * u + 1) * tok, :] = jnp.where(keep, high, 0.0).astype(BF)
        out_ref[(2 * u + 1) * tok : (2 * u + 2) * tok, :] = jnp.where(keep, low, 0.0).astype(BF)


def gates(routes_t, tokens, router_t):
    tok = tokens.shape[0]
    return pl.pallas_call(
        gates_kernel,
        out_shape=jax.ShapeDtypeStruct((2 * UNITS * tok, EXPERTS * 8), BF),
        in_specs=[VM, VM, VM],
        out_specs=VM,
        compiler_params=pltpu.CompilerParams(vmem_limit_bytes=16 << 20),
        cost_estimate=pl.CostEstimate(flops=10**8, bytes_accessed=2 * 10**6, transcendentals=0),
        name="gates",
    )(routes_t, tokens, router_t)


def pages_out_kernel(slot_ref, cache_ref, out_ref):
    pages, width = cache_ref.shape
    devices, chunks, _ = out_ref.shape
    chunk = width // chunks
    message = iota((devices, pages), 0)
    first = ((message & 7) * 16 + (message >> 3)) * pages
    slot = slot_ref[...]
    hit = (slot >= first) & (slot < first + pages)
    landing = jnp.sum(jnp.where(hit, slot - first + 1, 0), axis=1, keepdims=True)
    landing = jnp.broadcast_to(landing.astype(F32), (devices, 128))
    pick = onehot(hit)
    for c in range(chunks):
        got = jnp.dot(
            pick, cache_ref[:, c * chunk : (c + 1) * chunk], preferred_element_type=F32
        )
        out_ref[:, c, :chunk] = got.astype(BF)
        out_ref[:, c, chunk:] = landing.astype(BF)


def pages_out(slot_row, cache, devices):
    width = cache.shape[1]
    return pl.pallas_call(
        pages_out_kernel,
        out_shape=jax.ShapeDtypeStruct((devices, CHUNKS, width // CHUNKS + 128), BF),
        in_specs=[VM, VM],
        out_specs=VM,
        compiler_params=pltpu.CompilerParams(vmem_limit_bytes=40 << 20),
        cost_estimate=pl.CostEstimate(flops=2 * 10**9, bytes_accessed=4 * 10**6, transcendentals=0),
        name="pages_out",
    )(slot_row, cache)


def pages_in_kernel(got_ref, out_ref):
    pages, width = out_ref.shape
    devices, chunks, _ = got_ref.shape
    chunk = width // chunks
    landing = got_ref[:, 0, chunk:].astype(F32)
    square = jnp.where(iota((devices, 128), 0) == iota((devices, 128), 1), 1.0, 0.0)
    line = jnp.sum(landing * square, axis=0, keepdims=True).astype(jnp.int32)
    pick = onehot(line == iota((pages, devices), 0) + 1)
    for c in range(chunks):
        placed = jnp.dot(pick, got_ref[:, c, :chunk], preferred_element_type=F32)
        out_ref[:, c * chunk : (c + 1) * chunk] = placed.astype(BF)


def pages_in(got, pages, width):
    return pl.pallas_call(
        pages_in_kernel,
        out_shape=jax.ShapeDtypeStruct((pages, width), BF),
        in_specs=[VM],
        out_specs=VM,
        compiler_params=pltpu.CompilerParams(vmem_limit_bytes=16 << 20),
        cost_estimate=pl.CostEstimate(flops=2 * 10**9, bytes_accessed=4 * 10**6, transcendentals=0),
        name="pages_in",
    )(got)


def experts_kernel(x_ref, w_in_ref, w_out_ref, out_ref):
    rows, packed = x_ref.shape
    unit = packed // UNITS
    hidden = w_out_ref.shape[0]
    block = 128
    row, col = iota((block, UNITS * block), 0), iota((block, UNITS * block), 1)
    sub = row & 7
    inner = col & (block - 1)
    gather = onehot(
        (sub < CAPE)
        & ((row >> 3) == (inner >> 3))
        & ((col >> 7) == (sub >> 1))
        & ((inner & 7) == CAPE + (sub & 1))
    )
    row, col = iota((UNITS * block, block), 0), iota((UNITS * block, block), 1)
    sub = row & 7
    scatter = onehot(
        (sub >= CAPE)
        & (((row & (block - 1)) >> 3) == (col >> 3))
        & ((col & 7) == 2 * (row >> 7) + sub - CAPE)
    )
    tails = []
    for b in range(rows // block):
        part = x_ref[b * block : (b + 1) * block, :]
        part = jnp.concatenate([part[:, u * unit : (u + 1) * unit] for u in range(UNITS)], axis=0)
        tails.append(jnp.dot(gather, part, preferred_element_type=F32).astype(BF))
    tail = jnp.concatenate(tails, axis=0)
    gate_up = jnp.dot(x_ref[...], w_in_ref[: UNITS * unit, :], preferred_element_type=F32)
    gate_up = gate_up + jnp.dot(tail, w_in_ref[UNITS * unit :, :], preferred_element_type=F32)
    act = (jax.nn.silu(gate_up[:, :hidden]) * gate_up[:, hidden:]).astype(BF)
    y = jnp.dot(act, w_out_ref[...], preferred_element_type=F32)
    for b in range(rows // block):
        part = y[b * block : (b + 1) * block, :]
        moved = jnp.dot(scatter, part[:, UNITS * unit :].astype(BF), preferred_element_type=F32)
        keep = (iota((block, unit), 0) & 7) < CAPE
        for u in range(UNITS):
            out_ref[b * block : (b + 1) * block, u * unit : (u + 1) * unit] = jnp.where(
                keep, part[:, u * unit : (u + 1) * unit], moved[u * block : (u + 1) * block, :]
            ).astype(BF)


def experts(x, w_in, w_out):
    rows, packed = x.shape
    step = 256
    once = pl.Buffered(1)
    return pl.pallas_call(
        experts_kernel,
        grid=(rows // step,),
        out_shape=jax.ShapeDtypeStruct(x.shape, BF),
        in_specs=[
            pl.BlockSpec((step, packed), lambda i: (i, 0)),
            pl.BlockSpec(w_in.shape, lambda i: (0, 0), pipeline_mode=once),
            pl.BlockSpec(w_out.shape, lambda i: (0, 0), pipeline_mode=once),
        ],
        out_specs=pl.BlockSpec((step, packed), lambda i: (i, 0)),
        compiler_params=pltpu.CompilerParams(vmem_limit_bytes=40 << 20),
        cost_estimate=pl.CostEstimate(
            flops=10**10, bytes_accessed=15 * 10**6, transcendentals=10**6
        ),
        name="experts",
    )(x, w_in, w_out)


def combine_kernel(gate_hbm, got_ref, out_ref, gate_ref, sem):
    tok = out_ref.shape[0]
    unit = got_ref.shape[2] // UNITS
    loads = []
    for i, part in enumerate((slice(0, 2 * tok), slice(2 * tok, gate_ref.shape[0]))):
        load = pltpu.make_async_copy(gate_hbm.at[part], gate_ref.at[part], sem.at[i])
        load.start()
        loads.append(load)
    sums = []
    for u in range(UNITS):
        own = slice(u * unit, (u + 1) * unit)
        added = got_ref[:, :32, own].astype(F32) + got_ref[:, 32:, own].astype(F32)
        sums.append(added.astype(BF).reshape(-1, unit))
    loads[0].wait()
    both = gate_ref[0 : 2 * tok, :]
    is_main = (iota(both.shape, 1) & 7) < CAPE
    main = jnp.where(is_main, both, jnp.zeros_like(both))
    tail = jnp.where(is_main, jnp.zeros_like(both), both)
    total = jnp.zeros((2 * tok, unit), F32)
    for u in range(UNITS):
        if u == 1:
            loads[1].wait()
        if u > 0:
            tail = gate_ref[2 * tok * u : 2 * tok * (u + 1), :]
        both = jnp.dot(
            jnp.concatenate([main, tail], axis=0),
            sums[u],
            preferred_element_type=F32,
        )
        out_ref[:, u * unit : (u + 1) * unit] = (both[:tok] + both[tok : 2 * tok]).astype(BF)
        total = total + both[2 * tok :]
    out_ref[:, UNITS * unit :] = (total[:tok] + total[tok:]).astype(BF)


def combine(gate, got, tok, width):
    packed = got.shape[1]
    return pl.pallas_call(
        combine_kernel,
        out_shape=jax.ShapeDtypeStruct((tok, width), BF),
        in_specs=[pl.BlockSpec(memory_space=pltpu.HBM), VM],
        out_specs=VM,
        scratch_shapes=[
            pltpu.VMEM(gate.shape, BF),
            pltpu.SemaphoreType.DMA((2,)),
        ],
        compiler_params=pltpu.CompilerParams(vmem_limit_bytes=12 << 20),
        cost_estimate=pl.CostEstimate(flops=10**9, bytes_accessed=4 * 10**6, transcendentals=0),
        name="combine",
    )(pltpu.with_memory_space_constraint(gate, pltpu.HBM), got.reshape(16, 64, packed))


def swap(x):
    return lax.all_to_all(x, SWAP, split_axis=0, concat_axis=0, tiled=True)


def per_device(tokens, routes, router, w_in, w_out, cache_prefill, page_slot):
    devices = lax.axis_size("row") * lax.axis_size("col")
    pages = page_slot.shape[0]
    routes_t = routes.T
    arrived = swap(dispatch(routes_t, tokens))
    gate = gates(routes_t, tokens, router.T)
    moved = swap(pages_out(page_slot.reshape(1, pages), cache_prefill, devices))
    returned = swap(experts(arrived, w_in[0], w_out[0]))
    cache_decode = pages_in(moved, pages, cache_prefill.shape[1])
    moe_out = combine(gate, returned, tokens.shape[0], tokens.shape[1])
    return (moe_out, cache_decode)


def solution(mesh):
    in_specs = (
        P(AXES, None),
        P(AXES, None),
        P(),
        P(AXES, None, None),
        P(AXES, None, None),
        P(AXES, None),
        P(AXES),
    )
    out_specs = (P(AXES, None), P(AXES, None))
    return jax.shard_map(
        per_device, mesh=mesh, in_specs=in_specs, out_specs=out_specs, check_vma=False
    )
```

```python
import functools

import jax
import jax.numpy as jnp
from jax import lax
from jax.experimental import pallas as pl
from jax.experimental.pallas import tpu as pltpu
from jax.sharding import PartitionSpec as P

EXPERTS = 64
CAPE = 6
CHUNKS = 2
ROUTE_SCALE = 2.446
AXES = ("row", "col")
SWAP = ("col", "row")
BF = jnp.bfloat16
F32 = jnp.float32
VM = pl.BlockSpec(memory_space=pltpu.VMEM)


UNITS = 3


def iota(shape, dim):
    return lax.broadcasted_iota(jnp.int32, shape, dim)


def onehot(cond):
    return jnp.where(cond, 1.0, 0.0).astype(BF)


def slot_expert(row):
    return (((row >> 3) & 3) << 4) + (row >> 5)


def dispatch_kernel(routes_hbm, tok_hbm, out_hbm, routes_ref, tok_ref, buf_ref, in_sem, out_sem):
    tok = tok_ref.shape[0]
    rows = EXPERTS * 8
    unit = buf_ref.shape[3]
    load_routes = pltpu.make_async_copy(routes_hbm, routes_ref, in_sem.at[0])
    load_tok = pltpu.make_async_copy(tok_hbm, tok_ref, in_sem.at[1])
    load_routes.start()
    load_tok.start()
    load_routes.wait()
    row, col = iota((rows, 2 * tok), 0), iota((rows, 2 * tok), 1)
    expert, sub = slot_expert(row), row & 7
    routes = jnp.concatenate([routes_ref[...], routes_ref[...]], axis=1)
    named = routes[0:1, :] == expert
    for k in range(1, routes_ref.shape[0]):
        named = named | (routes[k : k + 1, :] == expert)
    first, second = iota((2 * tok, 2 * tok), 0), iota((2 * tok, 2 * tok), 1)
    before = onehot(first < jnp.where(second < tok, second, second - tok))
    rank = jnp.dot(onehot(named), before, preferred_element_type=F32).astype(jnp.int32)
    rank = jnp.where(named, rank, 99)
    load_tok.wait()
    last = tok_ref[:, UNITS * unit :]
    stores = []
    for u in range(UNITS):
        wanted = jnp.where(col < tok, sub, jnp.where(sub >= CAPE, sub + (2 * u - CAPE), -1))
        source = jnp.concatenate([tok_ref[:, u * unit : (u + 1) * unit], last], axis=0)
        picked = jnp.dot(onehot(rank == wanted), source, preferred_element_type=F32)
        buf_ref[u] = picked.astype(BF).reshape(buf_ref.shape[1:])
        for half in range(2):
            store = pltpu.make_async_copy(
                buf_ref.at[u],
                out_hbm.at[:, half, :, u * unit : (u + 1) * unit],
                out_sem.at[2 * u + half],
            )
            store.start()
            stores.append(store)
    for store in stores:
        store.wait()


def dispatch(routes_t, tokens):
    width = tokens.shape[1]
    unit = width * CAPE // 8 // UNITS
    hbm = pl.BlockSpec(memory_space=pltpu.HBM)
    out = pl.pallas_call(
        dispatch_kernel,
        out_shape=jax.ShapeDtypeStruct((16, 2, 32, UNITS * unit), BF),
        in_specs=[hbm, hbm],
        out_specs=hbm,
        scratch_shapes=[
            pltpu.VMEM(routes_t.shape, jnp.int32),
            pltpu.VMEM(tokens.shape, BF),
            pltpu.VMEM((UNITS, 16, 32, unit), BF),
            pltpu.SemaphoreType.DMA((2,)),
            pltpu.SemaphoreType.DMA((2 * UNITS,)),
        ],
        cost_estimate=pl.CostEstimate(flops=10**8, bytes_accessed=4 * 10**6, transcendentals=0),
        name="dispatch",
    )(routes_t, tokens)
    return out.reshape(2 * EXPERTS * 8, UNITS * unit)


def gates_kernel(routes_ref, tok_ref, router_ref, out_ref):
    tok = tok_ref.shape[0]
    cols = out_ref.shape[1]
    logits = lax.dot_general(
        tok_ref[...], router_ref[...], (((1,), (1,)), ((), ())), preferred_element_type=F32
    )
    scores = jax.nn.sigmoid(logits)
    expert = iota((EXPERTS, tok), 0)
    named = routes_ref[0:1, :] == expert
    for k in range(1, routes_ref.shape[0]):
        named = named | (routes_ref[k : k + 1, :] == expert)
    unit = onehot(iota((tok, tok), 0) == iota((tok, tok), 1))
    mine = lax.dot_general(
        unit, onehot(named), (((1,), (1,)), ((), ())), preferred_element_type=F32
    )
    before = onehot(iota((tok, tok), 1) < iota((tok, tok), 0))
    rank = jnp.dot(before, mine.astype(BF), preferred_element_type=F32)
    rank = jnp.where(mine > 0.5, rank, 99.0)
    picked = jnp.where(mine > 0.5, scores, 0.0)
    gate = ROUTE_SCALE * picked / jnp.sum(picked, axis=1, keepdims=True)
    high = gate.astype(BF)
    low = (gate - high.astype(F32)).astype(BF)
    spread = onehot(slot_expert(iota((EXPERTS, cols), 1)) == iota((EXPERTS, cols), 0))
    rank = jnp.dot(rank.astype(BF), spread, preferred_element_type=F32).astype(jnp.int32)
    high = jnp.dot(high, spread, preferred_element_type=F32)
    low = jnp.dot(low, spread, preferred_element_type=F32)
    sub = iota((tok, cols), 1) & 7
    for u in range(UNITS):
        keep = (sub >= CAPE) & (rank == sub + (2 * u - CAPE))
        if u == 0:
            keep = keep | (rank == sub)
        out_ref[2 * u * tok : (2 * u + 1) * tok, :] = jnp.where(keep, high, 0.0).astype(BF)
        out_ref[(2 * u + 1) * tok : (2 * u + 2) * tok, :] = jnp.where(keep, low, 0.0).astype(BF)


def gates(routes_t, tokens, router_t):
    tok = tokens.shape[0]
    return pl.pallas_call(
        gates_kernel,
        out_shape=jax.ShapeDtypeStruct((2 * UNITS * tok, EXPERTS * 8), BF),
        in_specs=[VM, VM, VM],
        out_specs=VM,
        compiler_params=pltpu.CompilerParams(vmem_limit_bytes=16 << 20),
        cost_estimate=pl.CostEstimate(flops=10**8, bytes_accessed=2 * 10**6, transcendentals=0),
        name="gates",
    )(routes_t, tokens, router_t)


def pages_out_kernel(slot_ref, cache_ref, out_ref):
    pages, width = cache_ref.shape
    devices, chunks, _ = out_ref.shape
    chunk = width // chunks
    message = iota((devices, pages), 0)
    first = ((message & 7) * 16 + (message >> 3)) * pages
    slot = slot_ref[...]
    hit = (slot >= first) & (slot < first + pages)
    landing = jnp.sum(jnp.where(hit, slot - first + 1, 0), axis=1, keepdims=True)
    landing = jnp.broadcast_to(landing.astype(F32), (devices, 128))
    pick = onehot(hit)
    for c in range(chunks):
        got = jnp.dot(
            pick, cache_ref[:, c * chunk : (c + 1) * chunk], preferred_element_type=F32
        )
        out_ref[:, c, :chunk] = got.astype(BF)
        out_ref[:, c, chunk:] = landing.astype(BF)


def pages_out(slot_row, cache, devices):
    width = cache.shape[1]
    return pl.pallas_call(
        pages_out_kernel,
        out_shape=jax.ShapeDtypeStruct((devices, CHUNKS, width // CHUNKS + 128), BF),
        in_specs=[VM, VM],
        out_specs=VM,
        compiler_params=pltpu.CompilerParams(vmem_limit_bytes=40 << 20),
        cost_estimate=pl.CostEstimate(flops=2 * 10**9, bytes_accessed=4 * 10**6, transcendentals=0),
        name="pages_out",
    )(slot_row, cache)


def pages_in_kernel(got_ref, out_ref):
    pages, width = out_ref.shape
    devices, chunks, _ = got_ref.shape
    chunk = width // chunks
    landing = got_ref[:, 0, chunk:].astype(F32)
    square = jnp.where(iota((devices, 128), 0) == iota((devices, 128), 1), 1.0, 0.0)
    line = jnp.sum(landing * square, axis=0, keepdims=True).astype(jnp.int32)
    pick = onehot(line == iota((pages, devices), 0) + 1)
    for c in range(chunks):
        placed = jnp.dot(pick, got_ref[:, c, :chunk], preferred_element_type=F32)
        out_ref[:, c * chunk : (c + 1) * chunk] = placed.astype(BF)


def pages_in(got, pages, width):
    return pl.pallas_call(
        pages_in_kernel,
        out_shape=jax.ShapeDtypeStruct((pages, width), BF),
        in_specs=[VM],
        out_specs=VM,
        compiler_params=pltpu.CompilerParams(vmem_limit_bytes=16 << 20),
        cost_estimate=pl.CostEstimate(flops=2 * 10**9, bytes_accessed=4 * 10**6, transcendentals=0),
        name="pages_in",
    )(got)


def experts_kernel(x_ref, w_in_ref, w_out_ref, out_ref):
    rows, packed = x_ref.shape
    unit = packed // UNITS
    hidden = w_out_ref.shape[0]
    block = 128
    row, col = iota((block, UNITS * block), 0), iota((block, UNITS * block), 1)
    sub = row & 7
    inner = col & (block - 1)
    gather = onehot(
        (sub < CAPE)
        & ((row >> 3) == (inner >> 3))
        & ((col >> 7) == (sub >> 1))
        & ((inner & 7) == CAPE + (sub & 1))
    )
    row, col = iota((UNITS * block, block), 0), iota((UNITS * block, block), 1)
    sub = row & 7
    scatter = onehot(
        (sub >= CAPE)
        & (((row & (block - 1)) >> 3) == (col >> 3))
        & ((col & 7) == 2 * (row >> 7) + sub - CAPE)
    )
    tails = []
    for b in range(rows // block):
        part = x_ref[b * block : (b + 1) * block, :]
        part = jnp.concatenate([part[:, u * unit : (u + 1) * unit] for u in range(UNITS)], axis=0)
        tails.append(jnp.dot(gather, part, preferred_element_type=F32).astype(BF))
    tail = jnp.concatenate(tails, axis=0)
    gate_up = jnp.dot(x_ref[...], w_in_ref[: UNITS * unit, :], preferred_element_type=F32)
    gate_up = gate_up + jnp.dot(tail, w_in_ref[UNITS * unit :, :], preferred_element_type=F32)
    act = (jax.nn.silu(gate_up[:, :hidden]) * gate_up[:, hidden:]).astype(BF)
    y = jnp.dot(act, w_out_ref[...], preferred_element_type=F32)
    for b in range(rows // block):
        part = y[b * block : (b + 1) * block, :]
        moved = jnp.dot(scatter, part[:, UNITS * unit :].astype(BF), preferred_element_type=F32)
        keep = (iota((block, unit), 0) & 7) < CAPE
        for u in range(UNITS):
            out_ref[b * block : (b + 1) * block, u * unit : (u + 1) * unit] = jnp.where(
                keep, part[:, u * unit : (u + 1) * unit], moved[u * block : (u + 1) * block, :]
            ).astype(BF)


def experts(x, w_in, w_out):
    rows, packed = x.shape
    step = 256
    once = pl.Buffered(1)
    return pl.pallas_call(
        experts_kernel,
        grid=(rows // step,),
        out_shape=jax.ShapeDtypeStruct(x.shape, BF),
        in_specs=[
            pl.BlockSpec((step, packed), lambda i: (i, 0)),
            pl.BlockSpec(w_in.shape, lambda i: (0, 0), pipeline_mode=once),
            pl.BlockSpec(w_out.shape, lambda i: (0, 0), pipeline_mode=once),
        ],
        out_specs=pl.BlockSpec((step, packed), lambda i: (i, 0)),
        compiler_params=pltpu.CompilerParams(vmem_limit_bytes=40 << 20),
        cost_estimate=pl.CostEstimate(
            flops=10**10, bytes_accessed=15 * 10**6, transcendentals=10**6
        ),
        name="experts",
    )(x, w_in, w_out)


def combine_kernel(gate_hbm, got_ref, out_ref, gate_ref, sem):
    tok = out_ref.shape[0]
    unit = got_ref.shape[2] // UNITS
    loads = []
    for i, part in enumerate((slice(0, 2 * tok), slice(2 * tok, gate_ref.shape[0]))):
        load = pltpu.make_async_copy(gate_hbm.at[part], gate_ref.at[part], sem.at[i])
        load.start()
        loads.append(load)
    sums = []
    for u in range(UNITS):
        own = slice(u * unit, (u + 1) * unit)
        sums.append((got_ref[:, :32, own] + got_ref[:, 32:, own]).reshape(-1, unit))
    loads[0].wait()
    both = gate_ref[0 : 2 * tok, :]
    is_main = (iota(both.shape, 1) & 7) < CAPE
    main = jnp.where(is_main, both, jnp.zeros_like(both))
    tail = jnp.where(is_main, jnp.zeros_like(both), both)
    total = jnp.zeros((2 * tok, unit), F32)
    for u in range(UNITS):
        if u == 1:
            loads[1].wait()
        if u > 0:
            tail = gate_ref[2 * tok * u : 2 * tok * (u + 1), :]
        both = jnp.dot(
            jnp.concatenate([main, tail], axis=0),
            sums[u],
            preferred_element_type=F32,
        )
        out_ref[:, u * unit : (u + 1) * unit] = (both[:tok] + both[tok : 2 * tok]).astype(BF)
        total = total + both[2 * tok :]
    out_ref[:, UNITS * unit :] = (total[:tok] + total[tok:]).astype(BF)


def combine(gate, got, tok, width):
    packed = got.shape[1]
    return pl.pallas_call(
        combine_kernel,
        out_shape=jax.ShapeDtypeStruct((tok, width), BF),
        in_specs=[pl.BlockSpec(memory_space=pltpu.HBM), VM],
        out_specs=VM,
        scratch_shapes=[
            pltpu.VMEM(gate.shape, BF),
            pltpu.SemaphoreType.DMA((2,)),
        ],
        compiler_params=pltpu.CompilerParams(vmem_limit_bytes=12 << 20),
        cost_estimate=pl.CostEstimate(flops=10**9, bytes_accessed=4 * 10**6, transcendentals=0),
        name="combine",
    )(pltpu.with_memory_space_constraint(gate, pltpu.HBM), got.reshape(16, 64, packed))


def swap(x):
    return lax.all_to_all(x, SWAP, split_axis=0, concat_axis=0, tiled=True)


def per_device(tokens, routes, router, w_in, w_out, cache_prefill, page_slot):
    devices = lax.axis_size("row") * lax.axis_size("col")
    pages = page_slot.shape[0]
    routes_t = routes.T
    arrived = swap(dispatch(routes_t, tokens))
    gate = gates(routes_t, tokens, router.T)
    moved = swap(pages_out(page_slot.reshape(1, pages), cache_prefill, devices))
    returned = swap(experts(arrived, w_in[0], w_out[0]))
    cache_decode = pages_in(moved, pages, cache_prefill.shape[1])
    moe_out = combine(gate, returned, tokens.shape[0], tokens.shape[1])
    return (moe_out, cache_decode)


def solution(mesh):
    in_specs = (
        P(AXES, None),
        P(AXES, None),
        P(),
        P(AXES, None, None),
        P(AXES, None, None),
        P(AXES, None),
        P(AXES),
    )
    out_specs = (P(AXES, None), P(AXES, None))
    return jax.shard_map(
        per_device, mesh=mesh, in_specs=in_specs, out_specs=out_specs, check_vma=False
    )
```
